768 devices in a mesh: dam: 128 (over x, z_lo, y), sec: 6 (over z_hi, core).
Axes of the slice: x: 4, y: 8, z: 12 (z_hi: 3, z_lo: 4; z = z_hi * 4 + z_lo), core: 2. Of those that a mesh axis runs over, the one named last changes fastest.
Arguments:
- segment_load: float32 [128, 6, 16, 1024], P('dam', 'sec')
- segment_mask: int32 [128, 6, 16, 16], P('dam', 'sec'), may hold values 0 or 1
- stiffness: float32 [128, 6, 16, 64, 448], P('dam', 'sec'), may hold values from -2 to 3, as said below
- block_cols: int32 [128, 6, 16, 7], P('dam', 'sec'), may hold values from 0 to 15, as said below
- capillary: float32 [128, 6, 16, 64], P('dam', 'sec'), may hold values from 0.25 to 2
- dirichlet_blocks: float32 [128, 6, 16, 64, 64], P('dam', 'sec'), may hold values from -1 to 1, as said below
- face_map: int32 [128, 6, 4, 8], P('dam', 'sec'), may hold values from 0 to 15, as said below
- face_weight: float32 [128, 6, 4, 512], P('dam', 'sec'), may hold values from 0 to 2, as said below
- corner_map: int32 [128, 6, 4], P('dam', 'sec'), may hold values from 0 to 15, as said below
- coarse_inverse: float32 [128, 1536, 1536], P('dam', 'sec'), may hold values from -1 to 1, as said below
Outputs:
- solution: float32 [128, 6, 16, 1024], P('dam', 'sec')
- residual: float32 [128, 6, 16, 1024], P('dam', 'sec')
The draws below stay inside these ranges and needn't reach their ends.
Inputs may be any that keep to these rules, and one draw needn't show every extreme that they name: `block_cols`: in each subdomain block b stores blocks b, b + o1, b - o1, b + o2, b - o2, b + o3, b - o3 (mod 16), for 3 distinct offsets o1, o2, o3 from 1 to 7 drawn per subdomain, in that order. The stiffness is symmetric, its off-diagonal entries of a row sum in magnitude to under 1.5, and its diagonal entries are 2 to 3. `dirichlet_blocks`: each block is symmetric and positive definite. `coarse_inverse`: each cross-section's matrix is symmetric and positive definite. `face_map`: the 8 blocks of a face are distinct; position p of a face meets position p of the neighbour's opposite face. `face_weight`: equal on the two sides of an interface, zero on faces with no neighbour. `corner_map`: distinct within a subdomain.
All inputs are finite; a program needn't handle non-finite values. No bound on the sum of `segment_mask` on one device may be relied on, other than what follows from the above.
Results may differ from the reference program's by a relative error of at most 0.00075.
Values sent between devices are 32-bit elements; how exact they have to be, the bound alone decides.
A program may use at most 32 MiB of HBM per device.

```python
import math
import jax
import jax.numpy as jnp
from jax import lax

NB = 16
BD = 64
RHS = 16
KB = 7
NC = 4
ITERS = 2
FB = 8
SD = 128
SS = 6
CO = 1536


def draw_segment_load(key, part):
    first = jax.random.fold_in(key, 0)
    shape = (SD, SS, NB, BD * RHS)
    scale = (3.0 ** (jnp.arange(SD).astype(jnp.float32) / (SD - 1))).reshape(SD, 1, 1, 1)
    return jax.random.normal(first, shape, jnp.float32) * scale


def stiff_offsets(key):
    keys = jax.random.split(jax.random.fold_in(key, 17), SD * SS)
    half = (KB - 1) // 2

    def single(subkey):
        return (1 + jax.random.permutation(subkey, NB // 2 - 1)[:half]).astype(jnp.int32)
    return jax.vmap(single)(keys).reshape(SD, SS, half)


def draw_block_cols(key, part):
    offsets = stiff_offsets(key)
    half = (KB - 1) // 2
    base = jnp.arange(NB).astype(jnp.int32)
    plus = (base[None, None, :, None] + offsets[:, :, None, :]) % NB
    minus = (base[None, None, :, None] - offsets[:, :, None, :] + NB) % NB
    paired = jnp.stack([plus, minus], axis=-1).reshape(SD, SS, NB, 2 * half)
    own = jnp.broadcast_to(base[None, None, :, None], (SD, SS, NB, 1))
    return jnp.concatenate([own, paired], axis=-1).astype(jnp.int32)


def draw_stiffness(key, part):
    offsets = stiff_offsets(key)
    half = (KB - 1) // 2
    amp = 1.5 / (KB * BD)
    keys = jax.random.split(jax.random.fold_in(key, 29), 3)
    side = jax.random.uniform(keys[0], (SD, SS, half, NB, BD, BD), jnp.float32, -amp, amp)
    inner_part = jax.random.uniform(keys[1], (SD, SS, NB, BD, BD), jnp.float32, -amp, amp)
    inner_part = 0.5 * (inner_part + jnp.swapaxes(inner_part, -1, -2))
    diag_vals = 2.0 + jax.random.uniform(keys[2], (SD, SS, NB, BD), jnp.float32)
    ident = jnp.arange(BD)[:, None] == jnp.arange(BD)[None, :]
    blocks = [jnp.where(ident, diag_vals[..., None], inner_part)]
    base = jnp.arange(NB).astype(jnp.int32)
    for which in range(half):
        upper = side[:, :, which]
        index = (base[None, None, :] - offsets[:, :, which][:, :, None] + NB) % NB
        lower = jnp.take_along_axis(upper, index[..., None, None], axis=2)
        blocks.append(upper)
        blocks.append(jnp.swapaxes(lower, -1, -2))
    stacked = jnp.stack(blocks, axis=4)
    return stacked.reshape(SD, SS, NB, BD, KB * BD)


def draw_dirichlet_blocks(key, part):
    first, second = jax.random.split(jax.random.fold_in(key, 61))
    off = jax.random.uniform(first, (SD, SS, NB, BD, BD), jnp.float32, -0.25 / BD, 0.25 / BD)
    off = 0.5 * (off + jnp.swapaxes(off, -1, -2))
    diag_vals = jax.random.uniform(second, (SD, SS, NB, BD), jnp.float32, 0.3, 0.6)
    ident = jnp.arange(BD)[:, None] == jnp.arange(BD)[None, :]
    return jnp.where(ident, diag_vals[..., None], off)


def draw_coarse_inverse(key, part):
    first, second = jax.random.split(jax.random.fold_in(key, 67))
    off = jax.random.uniform(first, (SD, CO, CO), jnp.float32, -0.4 / CO, 0.4 / CO)
    off = 0.5 * (off + jnp.swapaxes(off, -1, -2))
    diag_vals = jax.random.uniform(second, (SD, CO), jnp.float32, 0.5, 1.0)
    ident = jnp.arange(CO)[:, None] == jnp.arange(CO)[None, :]
    return jnp.where(ident, diag_vals[..., None], off)


def draw_face_map(key, part):
    keys = jax.random.split(jax.random.fold_in(key, 41), SD * SS * 4)

    def single(subkey):
        return jax.random.permutation(subkey, NB)[:FB].astype(jnp.int32)
    return jax.vmap(single)(keys).reshape(SD, SS, 4, FB)


def draw_corner_map(key, part):
    keys = jax.random.split(jax.random.fold_in(key, 43), SD * SS)

    def single(subkey):
        return jax.random.permutation(subkey, NB)[:NC].astype(jnp.int32)
    return jax.vmap(single)(keys).reshape(SD, SS, NC)


def draw_face_weight(key, part):
    first, second = jax.random.split(jax.random.fold_in(key, 53))
    low = math.log(0.5)
    high = math.log(2.0)
    along_dam = jnp.exp(jax.random.uniform(first, (SD - 1, SS, FB * BD), jnp.float32, low, high))
    along_sec = jnp.exp(jax.random.uniform(second, (SD, SS - 1, FB * BD), jnp.float32, low, high))
    zero_dam = jnp.zeros((1, SS, FB * BD), jnp.float32)
    zero_sec = jnp.zeros((SD, 1, FB * BD), jnp.float32)
    dam_low = jnp.concatenate([zero_dam, along_dam], axis=0)
    dam_up = jnp.concatenate([along_dam, zero_dam], axis=0)
    sec_low = jnp.concatenate([zero_sec, along_sec], axis=1)
    sec_up = jnp.concatenate([along_sec, zero_sec], axis=1)
    return jnp.stack([dam_low, dam_up, sec_low, sec_up], axis=2)


def place_ends(array, stream_key, low, largest):
    shape = array.shape
    index_at = [jax.random.randint(jax.random.fold_in(stream_key, axis), (), 0, shape[axis]) for axis in range(len(shape))]
    array = array.at[tuple(index_at)].set(low)
    longest = shape.index(max(shape))
    index_at[longest] = (index_at[longest] + 1) % shape[longest]
    return array.at[tuple(index_at)].set(largest)


def block_scale(rng, extent, pieces, low, high):
    gain = 1.0
    for dim, parts in pieces:
        draws = jax.random.uniform(jax.random.fold_in(jax.random.fold_in(rng, 6), dim), (parts,), jnp.float32, low / len(pieces), high / len(pieces))
        gain = gain * jnp.repeat(jnp.exp(draws), extent[dim] // parts).reshape((-1,) + (1,) * (len(extent) - 1 - dim))
    return gain


def setup_inputs(seed: int = 0) -> dict:
    arg_keys = jax.random.split(jax.random.key(seed), 11)
    segment_load = draw_segment_load(jax.random.fold_in(arg_keys[10], 71), 0)
    segment_mask = place_ends((jax.random.randint(arg_keys[1], (SD, SS, NB, RHS), 0, 4) < 3).astype(jnp.int32), jax.random.fold_in(arg_keys[1], 1), 0, 1)
    stiffness = draw_stiffness(jax.random.fold_in(arg_keys[10], 71), 0)
    block_cols = draw_block_cols(jax.random.fold_in(arg_keys[10], 71), 0)
    capillary = jnp.clip(jnp.exp(math.log(2.0) - 2.0794415 * jax.random.uniform(arg_keys[4], (SD, SS, NB, BD), jnp.float32) ** block_scale(arg_keys[4], (SD, SS, NB, BD), ((0, 128), (1, 6)), -0.2, 0.2)), 0.25, 2.0)
    dirichlet_blocks = draw_dirichlet_blocks(jax.random.fold_in(arg_keys[10], 71), 0)
    face_map = draw_face_map(jax.random.fold_in(arg_keys[10], 71), 0)
    face_weight = draw_face_weight(jax.random.fold_in(arg_keys[10], 71), 0)
    corner_map = draw_corner_map(jax.random.fold_in(arg_keys[10], 71), 0)
    coarse_inverse = draw_coarse_inverse(jax.random.fold_in(arg_keys[10], 71), 0)
    return dict(segment_load=segment_load, segment_mask=segment_mask, stiffness=stiffness, block_cols=block_cols, capillary=capillary, dirichlet_blocks=dirichlet_blocks, face_map=face_map, face_weight=face_weight, corner_map=corner_map, coarse_inverse=coarse_inverse)


HIGH = lax.Precision.HIGHEST


def local_product(stiff, cols, tang, field):
    nblk, bdof = tang.shape
    ncol = field.shape[1] // bdof
    gathered = field[cols].reshape(nblk, cols.shape[1] * bdof, ncol)
    prod = jnp.einsum("bde,bes->bds", stiff, gathered, precision=HIGH)
    prod = prod + tang[:, :, None] * field.reshape(nblk, bdof, ncol)
    return prod.reshape(nblk, bdof * ncol)


def take_rows(field, index):
    return field[index]


def add_rows(field, index, values):
    return field.at[index].add(values)


def operate(field, stiffness, block_cols, capillary, face_map, face_weight):
    local = jax.vmap(jax.vmap(local_product))(stiffness, block_cols, capillary, field)
    faces = jax.vmap(jax.vmap(take_rows))(field, face_map)
    zero_dam = jnp.zeros_like(faces[:1, :, 0])
    zero_sec = jnp.zeros_like(faces[:, :1, 2])
    below = jnp.concatenate([zero_dam, faces[:-1, :, 1]], axis=0)
    above = jnp.concatenate([faces[1:, :, 0], zero_dam], axis=0)
    left_sec = jnp.concatenate([zero_sec, faces[:, :-1, 3]], axis=1)
    right_sec = jnp.concatenate([faces[:, 1:, 2], zero_sec], axis=1)
    beside = jnp.stack([below, above, left_sec, right_sec], axis=2)
    weights = face_weight.reshape(SD, SS, 4, FB, BD, 1)
    term = (weights * (faces - beside).reshape(SD, SS, 4, FB, BD, RHS)).reshape(SD, SS, 4 * FB, BD * RHS)
    return jax.vmap(jax.vmap(add_rows))(local, face_map.reshape(SD, SS, 4 * FB), term)


def precondition(resid, dirichlet_blocks, corner_map, coarse_inverse):
    shaped = resid.reshape(SD, SS, NB, BD, RHS)
    outz = jnp.einsum("ijbde,ijbes->ijbds", dirichlet_blocks, shaped, precision=HIGH).reshape(SD, SS, NB, BD * RHS)
    corners = jax.vmap(jax.vmap(take_rows))(resid, corner_map)
    stacked = corners.reshape(SD, SS * NC * BD, RHS)
    correct = jnp.einsum("iqp,ips->iqs", coarse_inverse, stacked, precision=HIGH).reshape(SD, SS, NC, BD * RHS)
    return jax.vmap(jax.vmap(add_rows))(outz, corner_map, correct)


def inner(first, second):
    return (first * second).reshape(SD, SS, NB, BD, RHS).sum(axis=(0, 1, 2, 3))


def spread(coef):
    return jnp.tile(coef, BD)


def reference(segment_load, segment_mask, stiffness, block_cols, capillary, dirichlet_blocks, face_map, face_weight, corner_map, coarse_inverse):
    masked = segment_load.reshape(SD, SS, NB, BD, RHS) * segment_mask.astype(jnp.float32)[:, :, :, None, :]
    resid = masked.reshape(SD, SS, NB, BD * RHS)
    solution = jnp.zeros_like(resid)
    zvec = precondition(resid, dirichlet_blocks, corner_map, coarse_inverse)
    direction = zvec
    gamma = inner(resid, zvec)
    for step in range(ITERS):
        image = operate(direction, stiffness, block_cols, capillary, face_map, face_weight)
        delta = inner(direction, image)
        alpha = spread(gamma / delta)
        solution = solution + alpha * direction
        resid = resid - alpha * image
        if step + 1 < ITERS:
            zvec = precondition(resid, dirichlet_blocks, corner_map, coarse_inverse)
            gnew = inner(resid, zvec)
            direction = zvec + spread(gnew / gamma) * direction
            gamma = gnew
    return (solution, resid)
```

```python
import functools

import jax
import jax.numpy as jnp
from jax import lax
from jax.experimental import pallas as pl
from jax.experimental.pallas import tpu as pltpu
from jax.sharding import PartitionSpec as P

MESH = pl.DeviceIdType.MESH
f32, bf16, i32 = jnp.float32, jnp.bfloat16, jnp.int32
HIGH = lax.Precision.HIGHEST

SPLITS = {128: (4, 4, 8), 8: (2, 2, 2), 4: (1, 2, 2), 2: (1, 1, 2)}


def iota(shape, dim):
    return lax.broadcasted_iota(i32, shape, dim)


def split(a):
    hi = a.astype(bf16)
    return hi, (a - hi.astype(f32)).astype(bf16)


def nn(a, b):
    return jnp.dot(a, b, preferred_element_type=f32)


def nt(a, b, precision=None):
    return lax.dot_general(
        a, b, (((1,), (1,)), ((), ())), precision=precision, preferred_element_type=f32
    )


def roll(a, amount, axis):
    return pltpu.roll(a, amount % a.shape[axis], axis)


def swap8(tile):
    sub, grp = iota((8, 128), 0), iota((8, 128), 1) // 16
    for s in (1, 2, 4):
        up = roll(roll(tile, 16 * s, 1), -s, 0)
        down = roll(roll(tile, -16 * s, 1), s, 0)
        tile = jnp.where(((sub ^ grp) & s) == 0, tile, jnp.where((grp & s) != 0, up, down))
    return tile


def onehot(field, table, product):
    hi, lo = split(field)
    both = product(jnp.concatenate([hi, lo], axis=0), table)
    half = field.shape[0]
    return both[:half] + both[half:]


def weights_of(field):
    hi, lo = split(field)
    return [
        jnp.concatenate([hi[:, h * 128 : h * 128 + 128], lo[:, h * 128 : h * 128 + 128]], axis=1)
        for h in range(2)
    ]


def block_apply(a_hi, a_lo, weights):
    grp = iota((64, 128), 1) // 16
    halves = []
    for h in range(2):
        rows = pl.ds(512 * h, 512)
        w = weights(h)
        one = nn(a_hi[rows, :], w)
        two = nn(a_lo[rows, :], w[:, :128])
        out = one[:, :128] + one[:, 128:] + two
        acc = out[:64]
        for b in range(1, 8):
            acc = jnp.where(grp == b, out[64 * b : 64 * b + 64], acc)
        halves.append(acc)
    return jnp.concatenate(halves, axis=1)


def kernel(
    dims, load_h, mask_h, stiff_h, cols_h, cap_h, pre_h, fmap_h, fw_h, cmap_h, coarse_h,
    x_ref, r_ref,
    load_v, mask_v, stiff_v, cols_v, cap_v, pre_v, fmap_v, fw_v, cmap_v, coarse_v,
    k_hi, k_lo, p_hi, p_lo, cc, table_f, table_c, table_t, fw_rows, fw_full, wk, wc,
    ybuf, gbuf, nbuf, own_a, own_b, red_a, red_b,
    in_sem, y_send, y_recv, g_send, g_recv, a_send, a_recv, b_send, b_recv,
):
    nx, nzl, ny, nzh = dims
    plane, column = nx * ny, nzl * nzh * 2
    dam, sec = lax.axis_index("dam"), lax.axis_index("sec")
    ndam, nsec = nx * nzl * ny, nzh * 2
    xx, zl, yy = dam // (nzl * ny), (dam // ny) % nzl, dam % ny
    zc = ((sec // 2) * nzl + zl) * 2 + sec % 2

    def plane_id(k):
        px, py = (xx + k // ny) % nx, (yy + k % ny) % ny
        return ((px * nzl + zl) * ny + py, sec)

    def column_id(k):
        q = (zc + k) % column
        z = q // 2
        return ((xx * nzl + z % nzl) * ny + yy, (z // nzl) * 2 + q % 2)

    face_ids = (
        ((dam + ndam - 1) % ndam, sec),
        ((dam + 1) % ndam, sec),
        (dam, (sec + nsec - 1) % nsec),
        (dam, (sec + 1) % nsec),
    )

    pairs = (
        (load_h, load_v), (mask_h, mask_v), (cmap_h, cmap_v), (pre_h, pre_v), (coarse_h, coarse_v),
        (fmap_h, fmap_v), (fw_h, fw_v), (cols_h, cols_v), (cap_h, cap_v), (stiff_h, stiff_v),
    )
    loads = [pltpu.make_async_copy(a, b, in_sem.at[n]) for n, (a, b) in enumerate(pairs)]
    for copy in loads:
        copy.start()

    barrier = pltpu.get_barrier_semaphore()

    def greet(target):
        pl.semaphore_signal(barrier, inc=1, device_id=target, device_id_type=MESH)

    greet(face_ids[0])
    greet(face_ids[1])
    lax.fori_loop(1, column, lambda k, c: (greet(column_id(k)), c)[1], 0)
    lax.fori_loop(1, plane, lambda k, c: (greet(plane_id(k)), c)[1], 0)

    lane = iota((8, 128), 1)
    grp8 = lane // 16

    loads[2].wait()
    loads[1].wait()
    loads[0].wait()
    row128 = iota((256, 128), 0)
    lane1, grp1 = iota((1, 128), 1), iota((1, 128), 1) // 16
    corner = cmap_v[...]
    where_c = jnp.zeros((1, 128), i32)
    for n in range(4):
        where_c = jnp.where(
            grp1 % 4 == n, jnp.broadcast_to(corner[:, n : n + 1], (1, 128)), where_c
        )
    target = where_c * 16 + lane1 % 16
    table_c[...] = jnp.where(row128 == jnp.broadcast_to(target, (256, 128)), 1.0, 0.0).astype(bf16)

    fan = jnp.where(iota((16, 128), 1) % 16 == iota((16, 128), 0), 1.0, 0.0)
    mask = nn(mask_v[...].astype(f32), fan)
    halves = []
    for h in range(2):
        m = mask[8 * h : 8 * h + 8]
        halves.append(
            jnp.concatenate(
                [
                    swap8(load_v[pl.ds(8 * h, 8), pl.ds(128 * t, 128)] * m)
                    for t in range(8)
                ],
                axis=0,
            )
        )
    r0 = jnp.concatenate(halves, axis=1)

    low = iota((32, 128), 1) < 64

    def send_corners(rnd, field):
        both = onehot(field, table_c[...], nn)
        ybuf[rnd, sec] = jnp.where(low, both[:32], both[32:])

        def copy(k):
            return pltpu.make_async_remote_copy(
                src_ref=ybuf.at[rnd, sec],
                dst_ref=ybuf.at[rnd, sec],
                send_sem=y_send.at[rnd, k - 1],
                recv_sem=y_recv.at[rnd],
                device_id=(dam, (sec + k) % nsec),
                device_id_type=MESH,
            )

        copies = [copy(k) for k in range(1, nsec)]
        return copies

    def coarse(rnd):
        first, lane32 = iota((32, 128), 1) < 16, None
        for j in range(nsec):
            y = ybuf[rnd, j]
            turned = [y if g == 0 else roll(y, -16 * g, 1) for g in range(8)]
            for n in range(4):
                for dh in range(2):
                    g = dh * 4 + n
                    hi = turned[g].astype(bf16).astype(f32)
                    prev = turned[(g + 7) % 8]
                    lo = prev - prev.astype(bf16).astype(f32)
                    wc[pl.ds(j * 256 + n * 64 + dh * 32, 32), :] = jnp.where(first, hi, lo).astype(bf16)
        out = nn(cc[...], wc[...])
        out = out[:256] + out[256:]
        wide = jnp.concatenate([out[64 * n : 64 * n + 64] for n in range(4)], axis=1)
        return onehot(wide, table_t[...], nt)

    def wait_corners(rnd):
        part = ybuf.at[rnd, pl.ds(0, nsec - 1)]
        pltpu.make_async_copy(part, part, y_recv.at[rnd]).wait()

    def smooth(field):
        w = weights_of(field)
        return block_apply(p_hi, p_lo, lambda h: w[h])

    copies = send_corners(0, r0)
    pl.semaphore_wait(barrier, plane + column)
    for copy in copies:
        copy.start()
    pending = list(copies)

    loads[3].wait()
    for b in range(16):
        hi, lo = split(pre_v[b])
        p_hi[pl.ds(64 * b, 64), :] = hi
        p_lo[pl.ds(64 * b, 64), :] = lo
    z0 = smooth(r0)
    loads[4].wait()
    for n in range(4):
        hi, lo = split(coarse_v[pl.ds(64 * n, 64), :])
        cc[pl.ds(64 * n, 64), :] = hi
        cc[pl.ds(256 + 64 * n, 64), :] = lo
    for n in range(4):
        t = jnp.broadcast_to(corner[:, n : n + 1], (1, 128)) * 16 + lane1 % 16
        t = jnp.where(grp1 < 2, t, -1)
        table_t[:, pl.ds(128 * n, 128)] = jnp.where(
            row128 == jnp.broadcast_to(t, (256, 128)), 1.0, 0.0
        ).astype(bf16)
    loads[5].wait()
    fm = fmap_v[...]
    grp4 = iota((4, 128), 1) // 16
    where_f = jnp.zeros((4, 128), i32)
    for p in range(8):
        where_f = jnp.where(grp4 == p, jnp.broadcast_to(fm[:, p : p + 1], (4, 128)), where_f)
    where_f = where_f * 16 + iota((4, 128), 1) % 16
    for f in range(4):
        table_f[:, pl.ds(128 * f, 128)] = jnp.where(
            row128 == jnp.broadcast_to(where_f[f : f + 1], (256, 128)), 1.0, 0.0
        ).astype(bf16)
    loads[6].wait()
    for f in range(4):
        for p in range(8):
            q = 8 * f + p
            fw_rows[pl.ds(16 * q, 16), :] = jnp.broadcast_to(
                fw_v[f : f + 1, 64 * p : 64 * p + 64], (16, 64)
            )
    eye = jnp.where(iota((64, 64), 0) == iota((64, 64), 1), 1.0, 0.0)
    fw_full[...] = nt(eye, fw_rows[...], HIGH)
    loads[7].wait()
    offsets = [
        jnp.broadcast_to(jnp.broadcast_to(cols_v[k][:, 0:1], (1, 128)), (64, 128)) for k in (1, 3, 5)
    ]
    loads[8].wait()
    place = jnp.where(iota((64, 128), 0) == iota((64, 128), 1), 1.0, 0.0)
    cap = jnp.dot(cap_v[...], place, precision=HIGH, preferred_element_type=f32)
    loads[9].wait()
    on_diag = iota((64, 128), 0) == iota((64, 128), 1)
    for b in range(16):
        rows = pl.ds(64 * b, 64)
        for t in range(4):
            wide = 128 if t < 3 else 64
            piece = stiff_v[b, :, 128 * t : 128 * t + wide]
            if t == 0:
                piece = piece + jnp.where(on_diag, jnp.broadcast_to(cap[b : b + 1], (64, 128)), 0.0)
            hi, lo = split(piece)
            k_hi[rows, 128 * t : 128 * t + wide] = hi
            k_lo[rows, 128 * t : 128 * t + wide] = lo
    k_hi[:, 448:512] = jnp.zeros((1024, 64), bf16)
    k_lo[:, 448:512] = jnp.zeros((1024, 64), bf16)
    for h in range(2):
        wk[h, 448:512, :] = jnp.zeros((64, 256), bf16)

    lane64 = iota((64, 128), 1)

    def shifted(field, bits, sign):
        a, b = field[:, :128], field[:, 128:]
        for s in (1, 2, 4):
            ra, rb = roll(a, -sign * 16 * s, 1), roll(b, -sign * 16 * s, 1)
            same = lane64 < 128 - 16 * s if sign > 0 else lane64 >= 16 * s
            na, nb = jnp.where(same, ra, rb), jnp.where(same, rb, ra)
            on = (bits & s) != 0
            a, b = jnp.where(on, na, a), jnp.where(on, nb, b)
        return jnp.concatenate([a, b], axis=1)

    def send_faces(rnd, field):
        faces = onehot(field, table_f[...], nn)
        out = []
        for f in range(4):
            gbuf[rnd, f] = faces[:, 128 * f : 128 * f + 128]
        for f in (2, 3, 0, 1):
            out.append(
                pltpu.make_async_remote_copy(
                    src_ref=gbuf.at[rnd, f],
                    dst_ref=nbuf.at[rnd, f ^ 1],
                    send_sem=g_send.at[rnd, f],
                    recv_sem=g_recv.at[rnd, f ^ 1],
                    device_id=face_ids[f],
                    device_id_type=MESH,
                )
            )
            out[-1].start()
        return faces, out

    def stiff(field):
        chunks = [field]
        for bits in offsets:
            chunks += [shifted(field, bits, 1), shifted(field, bits, -1)]
        for k, chunk in enumerate(chunks):
            for h, w in enumerate(weights_of(chunk)):
                wk[h, pl.ds(64 * k, 64), :] = w
        return block_apply(k_hi, k_lo, lambda h: wk[h])

    def wait_faces(rnd, faces, copies):
        for copy in copies:
            copy.wait_recv()
        beside = jnp.concatenate([nbuf[rnd, f] for f in range(4)], axis=1)
        return onehot(fw_full[...] * (faces - beside), table_f[...], nt)

    def rows_of(dots):
        sub = iota((8, 128), 0)
        acc = jnp.zeros((8, 128), f32)
        for n, total in enumerate(dots):
            line = total[:, :128] + total[:, 128:]
            line = jnp.sum(line, axis=0, keepdims=True)
            acc = jnp.where(sub == n, jnp.broadcast_to(line, (8, 128)), acc)
        for s in (16, 32, 64):
            acc = acc + roll(acc, s, 1)
        return jnp.sum(jnp.where(sub == grp8, acc, 0.0), axis=0, keepdims=True)

    def exchange(src, dst, send_sem, recv_sem, target, count):
        def body(k, carry):
            pltpu.make_async_remote_copy(
                src_ref=src,
                dst_ref=dst.at[k - 1],
                send_sem=send_sem,
                recv_sem=recv_sem,
                device_id=target(k),
                device_id_type=MESH,
            ).start()
            return carry

        lax.fori_loop(1, count, body, 0)

    def start_sum(rnd, dots):
        own_a[rnd] = rows_of(dots)
        exchange(own_a.at[rnd], red_a.at[rnd], a_send.at[rnd], a_recv.at[rnd], plane_id, plane)

    def relay_sum(rnd):
        pltpu.make_async_copy(red_a.at[rnd], red_a.at[rnd], a_recv.at[rnd]).wait()
        own_b[rnd] = jnp.sum(red_a[rnd], axis=0) + own_a[rnd]
        exchange(own_b.at[rnd], red_b.at[rnd], b_send.at[rnd], b_recv.at[rnd], column_id, column)

    def end_sum(rnd, count):
        pltpu.make_async_copy(red_b.at[rnd], red_b.at[rnd], b_recv.at[rnd]).wait()
        total = jnp.broadcast_to(jnp.sum(red_b[rnd], axis=0) + own_b[rnd], (8, 128))
        sums = []
        for n in range(count):
            one = jnp.where(grp8 == n, total, 0.0)
            for s in (16, 32, 64):
                one = one + roll(one, s, 1)
            sums.append(one)
        return sums

    def wide(coef):
        one = jnp.broadcast_to(coef[0:1], (64, 128))
        return jnp.concatenate([one, one], axis=1)

    wait_corners(0)
    z0 = z0 + coarse(0)
    faces, copies = send_faces(0, z0)
    pending += copies
    w0 = stiff(z0)
    w0 = w0 + wait_faces(0, faces, copies)

    copies = send_corners(1, w0)
    for copy in copies:
        copy.start()
    pending += copies
    start_sum(0, [r0 * z0, z0 * w0])
    q0 = smooth(w0)
    wait_corners(1)
    q0 = q0 + coarse(1)

    faces, copies = send_faces(1, q0)
    pending += copies
    relay_sum(0)
    s0 = stiff(q0)
    s0 = s0 + wait_faces(1, faces, copies)
    gamma, delta = end_sum(0, 2)
    alpha = gamma / delta
    wide_alpha = wide(alpha)
    r1 = r0 - wide_alpha * w0
    z1 = z0 - wide_alpha * q0
    az = w0 - wide_alpha * s0
    start_sum(1, [r1 * z1, z1 * az, z1 * w0 + z0 * az])

    def tiles(field):
        return [
            [swap8(field[8 * t : 8 * t + 8, 128 * h : 128 * h + 128]) for t in range(8)]
            for h in range(2)
        ]

    tz0, tz1 = tiles(z0), tiles(z1)
    relay_sum(1)
    tr1, taz, tw0 = tiles(r1), tiles(az), tiles(w0)
    gnew, e_zz, e_zw = end_sum(1, 3)
    beta = gnew / gamma
    alpha1 = gnew / (e_zz + beta * (e_zw + beta * delta))
    scaled = alpha1 * beta
    for h in range(2):
        for t in range(8):
            at = (pl.ds(8 * h, 8), pl.ds(128 * t, 128))
            x_ref[at] = (alpha + scaled) * tz0[h][t] + alpha1 * tz1[h][t]
            r_ref[at] = tr1[h][t] - alpha1 * taz[h][t] - scaled * tw0[h][t]

    for copy in pending:
        copy.wait_send()
    for rnd in range(2):
        pltpu.make_async_copy(red_a.at[rnd], red_a.at[rnd], a_send.at[rnd]).wait()
        pltpu.make_async_copy(red_b.at[rnd], red_b.at[rnd], b_send.at[rnd]).wait()


def solution(mesh):
    placed = (
        P("dam", "sec", None, None),
        P("dam", "sec", None, None),
        P("dam", "sec", None, None, None),
        P("dam", "sec", None, None),
        P("dam", "sec", None, None),
        P("dam", "sec", None, None, None),
        P("dam", "sec", None, None),
        P("dam", "sec", None, None),
        P("dam", "sec", None),
        P("dam", "sec", None),
    )
    dims = SPLITS[mesh.shape["dam"]] + (mesh.shape["sec"] // 2,)
    nx, nzl, ny, nzh = dims
    plane, column = nx * ny, nzl * nzh * 2

    def shards(load, mask, stiff, cols, cap, pre, fmap, fw, cmap, coarse):
        args = (
            load[0, 0], mask[0, 0], stiff[0, 0], cols[0, 0].T.reshape(7, 1, 16), cap[0, 0],
            pre[0, 0], fmap[0, 0], fw[0, 0], cmap[0], coarse[0],
        )
        vmem = pltpu.VMEM
        dma = pltpu.SemaphoreType.DMA
        scratch = [vmem(a.shape, a.dtype) for a in args] + [
            vmem((1024, 512), bf16), vmem((1024, 512), bf16),
            vmem((1024, 64), bf16), vmem((1024, 64), bf16),
            vmem((512, 1536), bf16),
            vmem((256, 512), bf16), vmem((256, 128), bf16), vmem((256, 512), bf16),
            vmem((512, 64), f32), vmem((64, 512), f32),
            vmem((2, 512, 256), bf16), vmem((1536, 128), bf16),
            vmem((2, 2 * nzh, 32, 128), f32),
            vmem((2, 4, 64, 128), f32), vmem((2, 4, 64, 128), f32),
            vmem((2, 1, 128), f32), vmem((2, 1, 128), f32),
            vmem((2, plane - 1, 1, 128), f32), vmem((2, column - 1, 1, 128), f32),
            dma((10,)),
            dma((2, 2 * nzh - 1)), dma((2,)),
            dma((2, 4)), dma((2, 4)),
            dma((2,)), dma((2,)), dma((2,)), dma((2,)),
        ]
        x, r = pl.pallas_call(
            functools.partial(kernel, dims),
            out_shape=[jax.ShapeDtypeStruct((16, 1024), f32)] * 2,
            in_specs=[pl.BlockSpec(memory_space=pl.ANY)] * 10,
            out_specs=[pl.BlockSpec(memory_space=pltpu.VMEM)] * 2,
            scratch_shapes=scratch,
            compiler_params=pltpu.CompilerParams(
                collective_id=0, has_side_effects=True, vmem_limit_bytes=48 * 1024 * 1024
            ),
        )(*args)
        return x[None, None], r[None, None]

    return jax.shard_map(
        shards,
        mesh=mesh,
        in_specs=placed,
        out_specs=(P("dam", "sec", None, None), P("dam", "sec", None, None)),
        check_vma=False,
    )
```

```python
import functools

import jax
import jax.numpy as jnp
from jax import lax
from jax.experimental import pallas as pl
from jax.experimental.pallas import tpu as pltpu
from jax.sharding import PartitionSpec as P

MESH = pl.DeviceIdType.MESH
f32, bf16, i32 = jnp.float32, jnp.bfloat16, jnp.int32
HIGH = lax.Precision.HIGHEST

SPLITS = {128: (4, 4, 8), 8: (2, 2, 2), 4: (1, 2, 2), 2: (1, 1, 2)}


def iota(shape, dim):
    return lax.broadcasted_iota(i32, shape, dim)


def split(a):
    hi = a.astype(bf16)
    return hi, (a - hi.astype(f32)).astype(bf16)


def nn(a, b):
    return jnp.dot(a, b, preferred_element_type=f32)


def nt(a, b, precision=None):
    return lax.dot_general(
        a, b, (((1,), (1,)), ((), ())), precision=precision, preferred_element_type=f32
    )


def roll(a, amount, axis):
    return pltpu.roll(a, amount % a.shape[axis], axis)


def swap8(tile):
    sub, grp = iota((8, 128), 0), iota((8, 128), 1) // 16
    for s in (1, 2, 4):
        up = roll(roll(tile, 16 * s, 1), -s, 0)
        down = roll(roll(tile, -16 * s, 1), s, 0)
        tile = jnp.where(((sub ^ grp) & s) == 0, tile, jnp.where((grp & s) != 0, up, down))
    return tile


def onehot(field, table, product):
    hi, lo = split(field)
    both = product(jnp.concatenate([hi, lo], axis=0), table)
    half = field.shape[0]
    return both[:half] + both[half:]


def weights_of(field):
    hi, lo = split(field)
    return [
        jnp.concatenate([hi[:, h * 128 : h * 128 + 128], lo[:, h * 128 : h * 128 + 128]], axis=1)
        for h in range(2)
    ]


def block_apply(a_hi, a_lo, weights):
    grp = iota((64, 128), 1) // 16
    halves = []
    for h in range(2):
        rows = pl.ds(512 * h, 512)
        w = weights(h)
        one = nn(a_hi[rows, :], w)
        two = nn(a_lo[rows, :], w[:, :128])
        out = one[:, :128] + one[:, 128:] + two
        acc = out[:64]
        for b in range(1, 8):
            acc = jnp.where(grp == b, out[64 * b : 64 * b + 64], acc)
        halves.append(acc)
    return jnp.concatenate(halves, axis=1)


def kernel(
    dims, load_h, mask_h, stiff_h, cols_h, cap_h, pre_h, fmap_h, fw_h, cmap_h, coarse_h,
    out_ref,
    load_v, mask_v, stiff_v, cols_v, cap_v, pre_v, fmap_v, fw_v, cmap_v, coarse_v,
    k_hi, k_lo, p_hi, p_lo, cc, table_f, table_c, table_t, table_tf, table_fc, fw_rows, fw_full, wk, wc,
    ybuf, gbuf, nbuf, own_a, own_b, red_a, red_b,
    in_sem, y_send, y_recv, g_send, g_recv, a_send, a_recv, b_send, b_recv,
):
    nx, nzl, ny, nzh = dims
    plane, column = nx * ny, nzl * nzh * 2
    dam, sec = lax.axis_index("dam"), lax.axis_index("sec")
    ndam, nsec = nx * nzl * ny, nzh * 2
    xx, zl, yy = dam // (nzl * ny), (dam // ny) % nzl, dam % ny
    zc = ((sec // 2) * nzl + zl) * 2 + sec % 2

    def plane_id(k):
        px, py = (xx + k // ny) % nx, (yy + k % ny) % ny
        return ((px * nzl + zl) * ny + py, sec)

    def column_id(k):
        q = (zc + k) % column
        z = q // 2
        return ((xx * nzl + z % nzl) * ny + yy, (z // nzl) * 2 + q % 2)

    face_ids = (
        ((dam + ndam - 1) % ndam, sec),
        ((dam + 1) % ndam, sec),
        (dam, (sec + nsec - 1) % nsec),
        (dam, (sec + 1) % nsec),
    )

    pairs = (
        (load_h, load_v), (mask_h, mask_v), (cmap_h, cmap_v), (pre_h, pre_v), (coarse_h, coarse_v),
        (fmap_h, fmap_v), (fw_h, fw_v), (cols_h, cols_v), (cap_h, cap_v), (stiff_h, stiff_v),
    )
    loads = [pltpu.make_async_copy(a, b, in_sem.at[n]) for n, (a, b) in enumerate(pairs)]
    for copy in loads[:3]:
        copy.start()

    barrier = pltpu.get_barrier_semaphore()

    def greet(target):
        pl.semaphore_signal(barrier, inc=1, device_id=target, device_id_type=MESH)

    below, above = dam > 0, dam < ndam - 1
    column_ids = [column_id(k) for k in range(1, column)]
    plane_ids = [plane_id(k) for k in range(1, plane)]
    for target in column_ids + plane_ids:
        greet(target)
    pl.when(below)(lambda: greet(face_ids[0]))
    pl.when(above)(lambda: greet(face_ids[1]))
    for copy in loads[3:]:
        copy.start()

    lane = iota((8, 128), 1)
    grp8 = lane // 16

    loads[2].wait()
    loads[1].wait()
    loads[0].wait()
    row128 = iota((256, 128), 0)
    lane1, grp1 = iota((1, 128), 1), iota((1, 128), 1) // 16
    corner = cmap_v[...]
    where_c = jnp.zeros((1, 128), i32)
    for n in range(4):
        where_c = jnp.where(
            grp1 % 4 == n, jnp.broadcast_to(corner[:, n : n + 1], (1, 128)), where_c
        )
    target = where_c * 16 + lane1 % 16
    table_c[...] = jnp.where(row128 == jnp.broadcast_to(target, (256, 128)), 1.0, 0.0).astype(bf16)

    fan = jnp.where(iota((16, 128), 1) % 16 == iota((16, 128), 0), 1.0, 0.0)
    mask = nn(mask_v[...].astype(f32), fan)
    halves = []
    for h in range(2):
        m = mask[8 * h : 8 * h + 8]
        halves.append(
            jnp.concatenate(
                [
                    swap8(load_v[pl.ds(8 * h, 8), pl.ds(128 * t, 128)] * m)
                    for t in range(8)
                ],
                axis=0,
            )
        )
    r0 = jnp.concatenate(halves, axis=1)

    low = iota((32, 128), 1) < 64
    zh, core = sec // 2, sec % 2

    def corner_copies(rnd):
        def copy(dz, rc):
            return pltpu.make_async_remote_copy(
                src_ref=ybuf.at[rnd, sec],
                dst_ref=ybuf.at[rnd, sec],
                send_sem=y_send.at[rnd, 2 * dz + rc - 1],
                recv_sem=y_recv.at[rnd, dz],
                device_id=(dam, ((zh + dz) % nzh) * 2 + (core + rc) % 2),
                device_id_type=MESH,
            )

        return [copy(dz, rc) for dz in range(1, nzh) for rc in range(2)] + [copy(0, 1)]

    def put_corners(rnd, both):
        ybuf[rnd, sec] = jnp.where(low, both[:32], both[32:])

    def coarse_part(rnd, dz):
        count = 2 if dz else 1
        part = ybuf.at[rnd, pl.ds(0, count)]
        pltpu.make_async_copy(part, part, y_recv.at[rnd, dz]).wait()
        chip = (zh + nzh - dz) % nzh
        first = iota((32, 128), 1) < 16
        for c in range(2):
            y = ybuf[rnd, 2 * chip + c]
            turned = [y if g == 0 else roll(y, -16 * g, 1) for g in range(8)]
            for n in range(4):
                for dh in range(2):
                    g = dh * 4 + n
                    hi = turned[g].astype(bf16).astype(f32)
                    prev = turned[(g + 7) % 8]
                    lo = prev - prev.astype(bf16).astype(f32)
                    wc[dz, pl.ds(c * 256 + n * 64 + dh * 32, 32), :] = jnp.where(first, hi, lo).astype(bf16)
        return nn(cc[:, pl.ds(pl.multiple_of(chip * 512, 512), 512)], wc[dz])

    def coarse_rest(rnd, out):
        for dz in range(1, nzh):
            out = out + coarse_part(rnd, dz)
        out = out[:256] + out[256:]
        wide = jnp.concatenate([out[64 * n : 64 * n + 64] for n in range(4)], axis=1)
        hi, lo = split(wide)
        return jnp.concatenate([hi, lo], axis=0)

    def fold(both):
        return both[:64] + both[64:]

    def smooth(field):
        w = weights_of(field)
        return block_apply(p_hi, p_lo, lambda h: w[h])

    put_corners(0, onehot(r0, table_c[...], nn))
    copies = corner_copies(0)
    pl.semaphore_wait(barrier, plane + column - 2 + below.astype(i32) + above.astype(i32))
    for copy in copies:
        copy.start()
    pending = list(copies)

    loads[3].wait()
    for b in range(16):
        hi, lo = split(pre_v[b])
        p_hi[pl.ds(64 * b, 64), :] = hi
        p_lo[pl.ds(64 * b, 64), :] = lo
    z0 = smooth(r0)
    loads[4].wait()
    for n in range(4):
        hi, lo = split(coarse_v[pl.ds(64 * n, 64), :])
        cc[pl.ds(64 * n, 64), :] = hi
        cc[pl.ds(256 + 64 * n, 64), :] = lo
    for n in range(4):
        t = jnp.broadcast_to(corner[:, n : n + 1], (1, 128)) * 16 + lane1 % 16
        t = jnp.where(grp1 < 2, t, -1)
        table_t[:, pl.ds(128 * n, 128)] = jnp.where(
            row128 == jnp.broadcast_to(t, (256, 128)), 1.0, 0.0
        ).astype(bf16)
    loads[5].wait()
    fm = fmap_v[...]
    grp4 = iota((4, 128), 1) // 16
    where_f = jnp.zeros((4, 128), i32)
    for p in range(8):
        where_f = jnp.where(grp4 == p, jnp.broadcast_to(fm[:, p : p + 1], (4, 128)), where_f)
    where_f = where_f * 16 + iota((4, 128), 1) % 16
    for f in range(4):
        table_f[:, pl.ds(128 * f, 128)] = jnp.where(
            row128 == jnp.broadcast_to(where_f[f : f + 1], (256, 128)), 1.0, 0.0
        ).astype(bf16)
    modrow = iota((128, 128), 0) % 16
    rown = (iota((128, 128), 0) // 16) % 4
    early = iota((128, 128), 0) < 32
    for f in range(4):
        lanes = where_f[f : f + 1]
        match = jnp.zeros((128, 128), i32)
        for n in range(4):
            t = jnp.where(
                lanes // 16 == jnp.broadcast_to(corner[:, n : n + 1], (1, 128)), lane1 % 16, -1
            )
            t = jnp.broadcast_to(t, (128, 128))
            match = jnp.where(rown == n, t, match)
            table_tf[pl.ds(128 * n, 128), pl.ds(128 * f, 128)] = jnp.where(
                early, jnp.where(modrow == t, 1.0, 0.0), 0.0
            ).astype(bf16)
        table_fc[:, pl.ds(128 * f, 128)] = jnp.where(modrow == match, 1.0, 0.0).astype(bf16)
    loads[6].wait()
    for f in range(4):
        for p in range(8):
            q = 8 * f + p
            fw_rows[pl.ds(16 * q, 16), :] = jnp.broadcast_to(
                fw_v[f : f + 1, 64 * p : 64 * p + 64], (16, 64)
            )
    eye = jnp.where(iota((64, 64), 0) == iota((64, 64), 1), 1.0, 0.0)
    fw_full[...] = nt(eye, fw_rows[...], HIGH)
    loads[7].wait()
    offsets = [
        jnp.broadcast_to(jnp.broadcast_to(cols_v[k][:, 0:1], (1, 128)), (64, 128)) for k in (1, 3, 5)
    ]
    loads[8].wait()
    place = jnp.where(iota((64, 128), 0) == iota((64, 128), 1), 1.0, 0.0)
    cap = jnp.dot(cap_v[...], place, precision=HIGH, preferred_element_type=f32)
    loads[9].wait()
    on_diag = iota((64, 128), 0) == iota((64, 128), 1)
    for b in range(16):
        rows = pl.ds(64 * b, 64)
        for t in range(4):
            wide = 128 if t < 3 else 64
            piece = stiff_v[b, :, 128 * t : 128 * t + wide]
            if t == 0:
                piece = piece + jnp.where(on_diag, jnp.broadcast_to(cap[b : b + 1], (64, 128)), 0.0)
            hi, lo = split(piece)
            k_hi[rows, 128 * t : 128 * t + wide] = hi
            k_lo[rows, 128 * t : 128 * t + wide] = lo
    k_hi[:, 448:512] = jnp.zeros((1024, 64), bf16)
    k_lo[:, 448:512] = jnp.zeros((1024, 64), bf16)
    for h in range(2):
        wk[h, 448:512, :] = jnp.zeros((64, 256), bf16)

    lane64 = iota((64, 128), 1)

    def shifted(field, bits, sign):
        a, b = field[:, :128], field[:, 128:]
        for s in (1, 2, 4):
            ra, rb = roll(a, -sign * 16 * s, 1), roll(b, -sign * 16 * s, 1)
            same = lane64 < 128 - 16 * s if sign > 0 else lane64 >= 16 * s
            na, nb = jnp.where(same, ra, rb), jnp.where(same, rb, ra)
            on = (bits & s) != 0
            a, b = jnp.where(on, na, a), jnp.where(on, nb, b)
        return jnp.concatenate([a, b], axis=1)

    def face_copy(rnd, f):
        return pltpu.make_async_remote_copy(
            src_ref=gbuf.at[rnd, f],
            dst_ref=nbuf.at[rnd, f ^ 1],
            send_sem=g_send.at[rnd, f],
            recv_sem=g_recv.at[rnd, f ^ 1],
            device_id=face_ids[f],
            device_id_type=MESH,
        )

    def send_faces(rnd, faces):
        for f in range(4):
            gbuf[rnd, f] = faces[:, 128 * f : 128 * f + 128]
        face_copy(rnd, 2).start()
        face_copy(rnd, 3).start()
        pl.when(below)(lambda: face_copy(rnd, 0).start())
        pl.when(above)(lambda: face_copy(rnd, 1).start())

    def stiff(field):
        chunks = [field]
        for bits in offsets:
            chunks += [shifted(field, bits, 1), shifted(field, bits, -1)]
        for k, chunk in enumerate(chunks):
            for h, w in enumerate(weights_of(chunk)):
                wk[h, pl.ds(64 * k, 64), :] = w
        return block_apply(k_hi, k_lo, lambda h: wk[h])

    def wait_faces(rnd, faces):
        pl.when(above)(lambda: face_copy(rnd, 0).wait_recv())
        pl.when(below)(lambda: face_copy(rnd, 1).wait_recv())
        face_copy(rnd, 2).wait_recv()
        face_copy(rnd, 3).wait_recv()
        beside = jnp.concatenate([nbuf[rnd, f] for f in range(4)], axis=1)
        hi, lo = split(fw_full[...] * (faces - beside))
        return jnp.concatenate([hi, lo], axis=0)

    def rows_of(dots):
        sub = iota((8, 128), 0)
        acc = jnp.zeros((8, 128), f32)
        for n, total in enumerate(dots):
            line = total[:, :128] + total[:, 128:]
            line = jnp.sum(line, axis=0, keepdims=True)
            acc = jnp.where(sub == n, jnp.broadcast_to(line, (8, 128)), acc)
        for s in (16, 32, 64):
            acc = acc + roll(acc, s, 1)
        return jnp.sum(jnp.where(sub == grp8, acc, 0.0), axis=0, keepdims=True)

    def exchange(src, dst, send_sem, recv_sem, targets):
        for k, target in enumerate(targets):
            pltpu.make_async_remote_copy(
                src_ref=src,
                dst_ref=dst.at[k],
                send_sem=send_sem,
                recv_sem=recv_sem,
                device_id=target,
                device_id_type=MESH,
            ).start()

    def start_sum(rnd, dots):
        own_a[rnd] = rows_of(dots)
        exchange(own_a.at[rnd], red_a.at[rnd], a_send.at[rnd], a_recv.at[rnd], plane_ids)

    def relay_sum(rnd):
        pltpu.make_async_copy(red_a.at[rnd], red_a.at[rnd], a_recv.at[rnd]).wait()
        own_b[rnd] = jnp.sum(red_a[rnd], axis=0) + own_a[rnd]
        exchange(own_b.at[rnd], red_b.at[rnd], b_send.at[rnd], b_recv.at[rnd], column_ids)

    def end_sum(rnd, count):
        pltpu.make_async_copy(red_b.at[rnd], red_b.at[rnd], b_recv.at[rnd]).wait()
        total = jnp.broadcast_to(jnp.sum(red_b[rnd], axis=0) + own_b[rnd], (8, 128))
        sums = []
        for n in range(count):
            one = jnp.where(grp8 == n, total, 0.0)
            for s in (16, 32, 64):
                one = one + roll(one, s, 1)
            sums.append(one)
        return sums

    def wide(coef):
        one = jnp.broadcast_to(coef[0:1], (64, 128))
        return jnp.concatenate([one, one], axis=1)

    def clear(f):
        for rnd in range(2):
            nbuf[rnd, f] = jnp.zeros((64, 128), f32)

    pl.when(dam == 0)(lambda: clear(0))
    pl.when(dam == ndam - 1)(lambda: clear(1))

    faces = onehot(z0, table_f[...], nn)
    part = coarse_part(0, 0)
    fix = coarse_rest(0, part)
    faces = faces + fold(nn(fix, table_tf[...]))
    send_faces(0, faces)
    z0 = z0 + fold(nt(fix, table_t[...]))
    w0 = stiff(z0)
    corners = onehot(w0, table_c[...], nn)
    term = wait_faces(0, faces)
    put_corners(1, corners + fold(nt(term, table_fc[...])))
    copies = corner_copies(1)
    for copy in copies:
        copy.start()
    pending += copies
    w0 = w0 + fold(nt(term, table_f[...]))

    start_sum(0, [r0 * z0, z0 * w0])
    q0 = smooth(w0)
    faces = onehot(q0, table_f[...], nn)
    part = coarse_part(1, 0)
    fix = coarse_rest(1, part)
    faces = faces + fold(nn(fix, table_tf[...]))
    send_faces(1, faces)
    relay_sum(0)

    q0 = q0 + fold(nt(fix, table_t[...]))
    s0 = stiff(q0)
    gamma, delta = end_sum(0, 2)
    alpha = gamma / delta
    wide_alpha = wide(alpha)
    r1 = r0 - wide_alpha * w0
    z1 = z0 - wide_alpha * q0
    rz, zw = r1 * z1, z1 * w0
    term = wait_faces(1, faces)
    az = w0 - wide_alpha * (s0 + fold(nt(term, table_f[...])))
    start_sum(1, [rz, z1 * az, zw + z0 * az])

    def tiles(field):
        return [
            [swap8(field[8 * t : 8 * t + 8, 128 * h : 128 * h + 128]) for t in range(8)]
            for h in range(2)
        ]

    tz0, tz1 = tiles(z0), tiles(z1)
    relay_sum(1)
    tr1, taz, tw0 = tiles(r1), tiles(az), tiles(w0)
    gnew, e_zz, e_zw = end_sum(1, 3)
    beta = gnew / gamma
    alpha1 = gnew / (e_zz + beta * (e_zw + beta * delta))
    scaled = alpha1 * beta
    for h in range(2):
        for t in range(8):
            at = (pl.ds(8 * h, 8), pl.ds(128 * t, 128))
            out_ref[(0,) + at] = (alpha + scaled) * tz0[h][t] + alpha1 * tz1[h][t]
            out_ref[(1,) + at] = tr1[h][t] - alpha1 * taz[h][t] - scaled * tw0[h][t]

    for copy in pending:
        copy.wait_send()
    for rnd in range(2):
        face_copy(rnd, 2).wait_send()
        face_copy(rnd, 3).wait_send()
        pl.when(below)(lambda: face_copy(rnd, 0).wait_send())
        pl.when(above)(lambda: face_copy(rnd, 1).wait_send())
    for rnd in range(2):
        pltpu.make_async_copy(red_a.at[rnd], red_a.at[rnd], a_send.at[rnd]).wait()
        pltpu.make_async_copy(red_b.at[rnd], red_b.at[rnd], b_send.at[rnd]).wait()


def solution(mesh):
    placed = (
        P("dam", "sec", None, None),
        P("dam", "sec", None, None),
        P("dam", "sec", None, None, None),
        P("dam", "sec", None, None),
        P("dam", "sec", None, None),
        P("dam", "sec", None, None, None),
        P("dam", "sec", None, None),
        P("dam", "sec", None, None),
        P("dam", "sec", None),
        P("dam", "sec", None),
    )
    dims = SPLITS[mesh.shape["dam"]] + (mesh.shape["sec"] // 2,)
    nx, nzl, ny, nzh = dims
    plane, column = nx * ny, nzl * nzh * 2

    def shards(load, mask, stiff, cols, cap, pre, fmap, fw, cmap, coarse):
        args = (
            load[0, 0], mask[0, 0], stiff[0, 0], cols.transpose(0, 3, 1, 2)[0], cap[0, 0],
            pre[0, 0], fmap[0, 0], fw[0, 0], cmap[0], coarse[0],
        )
        vmem = pltpu.VMEM
        dma = pltpu.SemaphoreType.DMA
        scratch = [vmem(a.shape, a.dtype) for a in args] + [
            vmem((1024, 512), bf16), vmem((1024, 512), bf16),
            vmem((1024, 64), bf16), vmem((1024, 64), bf16),
            vmem((512, 1536), bf16),
            vmem((256, 512), bf16), vmem((256, 128), bf16), vmem((256, 512), bf16),
            vmem((512, 512), bf16), vmem((128, 512), bf16),
            vmem((512, 64), f32), vmem((64, 512), f32),
            vmem((2, 512, 256), bf16), vmem((3, 512, 128), bf16),
            vmem((2, 2 * nzh, 32, 128), f32),
            vmem((2, 4, 64, 128), f32), vmem((2, 4, 64, 128), f32),
            vmem((2, 1, 128), f32), vmem((2, 1, 128), f32),
            vmem((2, plane - 1, 1, 128), f32), vmem((2, column - 1, 1, 128), f32),
            dma((10,)),
            dma((2, 2 * nzh - 1)), dma((2, nzh)),
            dma((2, 4)), dma((2, 4)),
            dma((2,)), dma((2,)), dma((2,)), dma((2,)),
        ]
        out = pl.pallas_call(
            functools.partial(kernel, dims),
            out_shape=jax.ShapeDtypeStruct((2, 16, 1024), f32),
            in_specs=[pl.BlockSpec(memory_space=pl.ANY)] * 10,
            out_specs=pl.BlockSpec(memory_space=pltpu.VMEM),
            scratch_shapes=scratch,
            compiler_params=pltpu.CompilerParams(
                collective_id=0, has_side_effects=True, vmem_limit_bytes=67043328
            ),
        )(*args)
        return out[0][None, None], out[1][None, None]

    return jax.shard_map(
        shards,
        mesh=mesh,
        in_specs=placed,
        out_specs=(P("dam", "sec", None, None), P("dam", "sec", None, None)),
        check_vma=False,
    )
```

```python
import functools

import jax
import jax.numpy as jnp
from jax import lax
from jax.experimental import pallas as pl
from jax.experimental.pallas import tpu as pltpu
from jax.sharding import PartitionSpec as P

MESH = pl.DeviceIdType.MESH
f32, bf16, i32 = jnp.float32, jnp.bfloat16, jnp.int32
HIGH = lax.Precision.HIGHEST

SPLITS = {128: (4, 4, 8), 8: (2, 2, 2), 4: (1, 2, 2), 2: (1, 1, 2)}


def iota(shape, dim):
    return lax.broadcasted_iota(i32, shape, dim)


def split(a):
    hi = a.astype(bf16)
    return hi, (a - hi.astype(f32)).astype(bf16)


def nn(a, b):
    return jnp.dot(a, b, preferred_element_type=f32)


def nt(a, b, precision=None):
    return lax.dot_general(
        a, b, (((1,), (1,)), ((), ())), precision=precision, preferred_element_type=f32
    )


def roll(a, amount, axis):
    return pltpu.roll(a, amount % a.shape[axis], axis)


def swap8(tile):
    sub, grp = iota((8, 128), 0), iota((8, 128), 1) // 16
    for s in (1, 2, 4):
        up = roll(roll(tile, 16 * s, 1), -s, 0)
        down = roll(roll(tile, -16 * s, 1), s, 0)
        tile = jnp.where(((sub ^ grp) & s) == 0, tile, jnp.where((grp & s) != 0, up, down))
    return tile


def onehot(field, table, product):
    hi, lo = split(field)
    both = product(jnp.concatenate([hi, lo], axis=0), table)
    half = field.shape[0]
    return both[:half] + both[half:]


def weights_of(field):
    hi, lo = split(field)
    return [
        jnp.concatenate([hi[:, h * 128 : h * 128 + 128], lo[:, h * 128 : h * 128 + 128]], axis=1)
        for h in range(2)
    ]


def block_apply(a_hi, a_lo, weights):
    grp = iota((64, 128), 1) // 16
    halves = []
    for h in range(2):
        rows = pl.ds(512 * h, 512)
        w = weights(h)
        one = nn(a_hi[rows, :], w)
        two = nn(a_lo[rows, :], w[:, :128])
        out = one[:, :128] + one[:, 128:] + two
        acc = out[:64]
        for b in range(1, 8):
            acc = jnp.where(grp == b, out[64 * b : 64 * b + 64], acc)
        halves.append(acc)
    return jnp.concatenate(halves, axis=1)


def kernel(
    dims, load_h, mask_h, stiff_h, cols_h, cap_h, pre_h, fmap_h, fw_h, cmap_h, coarse_h,
    out_ref,
    load_v, mask_v, stiff_v, cols_v, cap_v, pre_v, fmap_v, fw_v, cmap_v, coarse_v,
    k_hi, k_lo, p_hi, p_lo, cc, table_f, table_c, table_t, table_tf, table_fc, fw_rows, fw_full, wk, wc,
    ybuf, gbuf, nbuf, own_a, own_b, red_a, red_b, fields, turned,
    in_sem, y_send, y_recv, g_send, g_recv, a_send, a_recv, b_send, b_recv,
):
    nx, nzl, ny, nzh = dims
    plane, column = nx * ny, nzl * nzh * 2
    dam, sec = lax.axis_index("dam"), lax.axis_index("sec")
    ndam, nsec = nx * nzl * ny, nzh * 2
    xx, zl, yy = lax.div(dam, nzl * ny), lax.rem(lax.div(dam, ny), nzl), lax.rem(dam, ny)
    zh, core = lax.div(sec, 2), lax.rem(sec, 2)

    def turns(at, size):
        return [at] + [jnp.where(at + k < size, at + k, at + k - size) for k in range(1, size)]

    ring_y, ring_core = turns(yy, ny), turns(core, 2)
    ring_x = [x * (nzl * ny) for x in turns(xx, nx)]
    ring_zl, ring_zh = [z * ny for z in turns(zl, nzl)], [z * 2 for z in turns(zh, nzh)]
    plane_ids = [(x + zl * ny + y, sec) for x in ring_x for y in ring_y][1:]
    column_ids = [
        (ring_x[0] + z + yy, h + c) for h in ring_zh for z in ring_zl for c in ring_core
    ][1:]

    face_ids = (
        (jnp.where(dam > 0, dam - 1, ndam - 1), sec),
        (jnp.where(dam < ndam - 1, dam + 1, 0), sec),
        (dam, jnp.where(sec > 0, sec - 1, nsec - 1)),
        (dam, jnp.where(sec < nsec - 1, sec + 1, 0)),
    )

    pairs = (
        (load_h, load_v), (mask_h, mask_v), (cmap_h, cmap_v), (pre_h, pre_v), (coarse_h, coarse_v),
        (fmap_h, fmap_v), (fw_h, fw_v), (cols_h, cols_v), (cap_h, cap_v), (stiff_h, stiff_v),
    )
    loads = [pltpu.make_async_copy(a, b, in_sem.at[n]) for n, (a, b) in enumerate(pairs)]
    for copy in loads[:3]:
        copy.start()

    barrier = pltpu.get_barrier_semaphore()

    def greet(target):
        pl.semaphore_signal(barrier, inc=1, device_id=target, device_id_type=MESH)

    below, above = dam > 0, dam < ndam - 1
    for target in column_ids + plane_ids:
        greet(target)
    pl.when(below)(lambda: greet(face_ids[0]))
    pl.when(above)(lambda: greet(face_ids[1]))
    for copy in loads[3:]:
        copy.start()

    lane = iota((8, 128), 1)
    grp8 = lane // 16

    loads[2].wait()
    loads[1].wait()
    loads[0].wait()
    row128 = iota((256, 128), 0)
    lane1, grp1 = iota((1, 128), 1), iota((1, 128), 1) // 16
    corner = cmap_v[...]
    where_c = jnp.zeros((1, 128), i32)
    for n in range(4):
        where_c = jnp.where(
            grp1 % 4 == n, jnp.broadcast_to(corner[:, n : n + 1], (1, 128)), where_c
        )
    target = where_c * 16 + lane1 % 16
    table_c[...] = jnp.where(row128 == jnp.broadcast_to(target, (256, 128)), 1.0, 0.0).astype(bf16)

    fan = jnp.where(iota((16, 128), 1) % 16 == iota((16, 128), 0), 1.0, 0.0)
    mask = nn(mask_v[...].astype(f32), fan)
    halves = []
    for h in range(2):
        m = mask[8 * h : 8 * h + 8]
        halves.append(
            jnp.concatenate(
                [
                    swap8(load_v[pl.ds(8 * h, 8), pl.ds(128 * t, 128)] * m)
                    for t in range(8)
                ],
                axis=0,
            )
        )
    r0 = jnp.concatenate(halves, axis=1)

    low = iota((32, 128), 1) < 64

    def corner_copies(rnd):
        def copy(dz, rc):
            return pltpu.make_async_remote_copy(
                src_ref=ybuf.at[rnd, sec],
                dst_ref=ybuf.at[rnd, sec],
                send_sem=y_send.at[rnd, 2 * dz + rc - 1],
                recv_sem=y_recv.at[rnd, dz],
                device_id=(dam, ring_zh[dz] + ring_core[rc]),
                device_id_type=MESH,
            )

        return [copy(dz, rc) for dz in range(1, nzh) for rc in range(2)] + [copy(0, 1)]

    def put_corners(rnd, both):
        ybuf[rnd, sec] = jnp.where(low, both[:32], both[32:])

    def coarse_weights(rnd, dz):
        chip = zh if dz == 0 else lax.div(ring_zh[nzh - dz], 2)
        first = iota((32, 128), 1) < 16
        for c in range(2):
            y = ybuf[rnd, 2 * chip + c]
            turned = [y if g == 0 else roll(y, -16 * g, 1) for g in range(8)]
            for n in range(4):
                for dh in range(2):
                    g = dh * 4 + n
                    hi = turned[g].astype(bf16).astype(f32)
                    prev = turned[(g + 7) % 8]
                    lo = prev - prev.astype(bf16).astype(f32)
                    wc[dz, pl.ds(c * 256 + n * 64 + dh * 32, 32), :] = jnp.where(first, hi, lo).astype(bf16)
        return pl.ds(pl.multiple_of(chip * 512, 512), 512)

    def wait_corners(rnd, dz):
        part = ybuf.at[rnd, pl.ds(0, 2 if dz else 1)]
        pltpu.make_async_copy(part, part, y_recv.at[rnd, dz]).wait()

    def coarse_own(rnd):
        wait_corners(rnd, 0)
        at = coarse_weights(rnd, 0)
        return nn(cc[:256, at], wc[0]) + nn(cc[256:, at], wc[0])

    def coarse_rest(rnd, out):
        for dz in range(1, nzh):
            wait_corners(rnd, dz)
        at = [coarse_weights(rnd, dz) for dz in range(1, nzh)]
        parts = [nn(cc[:256, a], wc[n + 1]) for n, a in enumerate(at)]
        parts += [nn(cc[256:, a], wc[n + 1]) for n, a in enumerate(at)]
        out = out + sum(parts[1:], parts[0])
        wide = jnp.concatenate([out[64 * n : 64 * n + 64] for n in range(4)], axis=1)
        hi, lo = split(wide)
        return jnp.concatenate([hi, lo], axis=0)

    def fold(both):
        return both[:64] + both[64:]

    def smooth(field):
        w = weights_of(field)
        return block_apply(p_hi, p_lo, lambda h: w[h])

    put_corners(0, onehot(r0, table_c[...], nn))
    copies = corner_copies(0)
    pl.semaphore_wait(barrier, plane + column - 2 + below.astype(i32) + above.astype(i32))
    for copy in copies:
        copy.start()
    pending = list(copies)

    loads[3].wait()
    for b in range(16):
        hi, lo = split(pre_v[b])
        p_hi[pl.ds(64 * b, 64), :] = hi
        p_lo[pl.ds(64 * b, 64), :] = lo
    z0 = smooth(r0)
    loads[4].wait()
    for n in range(4):
        hi, lo = split(coarse_v[pl.ds(64 * n, 64), :])
        cc[pl.ds(64 * n, 64), :] = hi
        cc[pl.ds(256 + 64 * n, 64), :] = lo
    for n in range(4):
        t = jnp.broadcast_to(corner[:, n : n + 1], (1, 128)) * 16 + lane1 % 16
        t = jnp.where(grp1 < 2, t, -1)
        table_t[:, pl.ds(128 * n, 128)] = jnp.where(
            row128 == jnp.broadcast_to(t, (256, 128)), 1.0, 0.0
        ).astype(bf16)
    loads[5].wait()
    fm = fmap_v[...]
    grp4 = iota((4, 128), 1) // 16
    where_f = jnp.zeros((4, 128), i32)
    for p in range(8):
        where_f = jnp.where(grp4 == p, jnp.broadcast_to(fm[:, p : p + 1], (4, 128)), where_f)
    where_f = where_f * 16 + iota((4, 128), 1) % 16
    for f in range(4):
        table_f[:, pl.ds(128 * f, 128)] = jnp.where(
            row128 == jnp.broadcast_to(where_f[f : f + 1], (256, 128)), 1.0, 0.0
        ).astype(bf16)
    modrow = iota((128, 128), 0) % 16
    rown = (iota((128, 128), 0) // 16) % 4
    early = iota((128, 128), 0) < 32
    for f in range(4):
        lanes = where_f[f : f + 1]
        match = jnp.zeros((128, 128), i32)
        for n in range(4):
            t = jnp.where(
                lanes // 16 == jnp.broadcast_to(corner[:, n : n + 1], (1, 128)), lane1 % 16, -1
            )
            t = jnp.broadcast_to(t, (128, 128))
            match = jnp.where(rown == n, t, match)
            table_tf[pl.ds(128 * n, 128), pl.ds(128 * f, 128)] = jnp.where(
                early, jnp.where(modrow == t, 1.0, 0.0), 0.0
            ).astype(bf16)
        table_fc[:, pl.ds(128 * f, 128)] = jnp.where(modrow == match, 1.0, 0.0).astype(bf16)
    loads[6].wait()
    for f in range(4):
        for p in range(8):
            q = 8 * f + p
            fw_rows[pl.ds(16 * q, 16), :] = jnp.broadcast_to(
                fw_v[f : f + 1, 64 * p : 64 * p + 64], (16, 64)
            )
    eye = jnp.where(iota((64, 64), 0) == iota((64, 64), 1), 1.0, 0.0)
    fw_full[...] = nt(eye, fw_rows[...], HIGH)
    loads[7].wait()
    offsets = [
        jnp.broadcast_to(jnp.broadcast_to(cols_v[k][:, 0:1], (1, 128)), (64, 128)) for k in (1, 3, 5)
    ]
    loads[8].wait()
    place = jnp.where(iota((64, 128), 0) == iota((64, 128), 1), 1.0, 0.0)
    cap = jnp.dot(cap_v[...], place, precision=HIGH, preferred_element_type=f32)
    loads[9].wait()
    on_diag = iota((64, 128), 0) == iota((64, 128), 1)
    for b in range(16):
        rows = pl.ds(64 * b, 64)
        for t in range(4):
            wide = 128 if t < 3 else 64
            piece = stiff_v[b, :, 128 * t : 128 * t + wide]
            if t == 0:
                piece = piece + jnp.where(on_diag, jnp.broadcast_to(cap[b : b + 1], (64, 128)), 0.0)
            hi, lo = split(piece)
            k_hi[rows, 128 * t : 128 * t + wide] = hi
            k_lo[rows, 128 * t : 128 * t + wide] = lo
    k_hi[:, 448:512] = jnp.zeros((1024, 64), bf16)
    k_lo[:, 448:512] = jnp.zeros((1024, 64), bf16)
    for h in range(2):
        wk[h, 448:512, :] = jnp.zeros((64, 256), bf16)

    lane64 = iota((64, 128), 1)

    def shifted(field, bits, sign):
        a, b = field[:, :128], field[:, 128:]
        for s in (1, 2, 4):
            ra, rb = roll(a, -sign * 16 * s, 1), roll(b, -sign * 16 * s, 1)
            same = lane64 < 128 - 16 * s if sign > 0 else lane64 >= 16 * s
            na, nb = jnp.where(same, ra, rb), jnp.where(same, rb, ra)
            on = (bits & s) != 0
            a, b = jnp.where(on, na, a), jnp.where(on, nb, b)
        return jnp.concatenate([a, b], axis=1)

    def face_copy(rnd, f):
        return pltpu.make_async_remote_copy(
            src_ref=gbuf.at[rnd, f],
            dst_ref=nbuf.at[rnd, f ^ 1],
            send_sem=g_send.at[rnd, f],
            recv_sem=g_recv.at[rnd, f ^ 1],
            device_id=face_ids[f],
            device_id_type=MESH,
        )

    def send_faces(rnd, faces):
        for f in range(4):
            gbuf[rnd, f] = faces[:, 128 * f : 128 * f + 128]
        face_copy(rnd, 2).start()
        face_copy(rnd, 3).start()
        pl.when(below)(lambda: face_copy(rnd, 0).start())
        pl.when(above)(lambda: face_copy(rnd, 1).start())

    def stiff(field):
        chunks = [field]
        for bits in offsets:
            chunks += [shifted(field, bits, 1), shifted(field, bits, -1)]
        for k, chunk in enumerate(chunks):
            for h, w in enumerate(weights_of(chunk)):
                wk[h, pl.ds(64 * k, 64), :] = w
        return block_apply(k_hi, k_lo, lambda h: wk[h])

    def wait_faces(rnd, faces):
        pl.when(above)(lambda: face_copy(rnd, 0).wait_recv())
        pl.when(below)(lambda: face_copy(rnd, 1).wait_recv())
        face_copy(rnd, 2).wait_recv()
        face_copy(rnd, 3).wait_recv()
        beside = jnp.concatenate([nbuf[rnd, f] for f in range(4)], axis=1)
        return fw_full[...] * (faces - beside)

    def two(value):
        return jnp.concatenate(split(value), axis=0)

    def lump(prod):
        line = sum(prod[:, 128 * n : 128 * n + 128] for n in range(1, prod.shape[1] // 128))
        line = prod[:, :128] + line
        return sum((line[8 * t : 8 * t + 8] for t in range(1, 8)), line[:8])

    def rows_of(dots):
        sub = iota((8, 128), 0)
        acc = jnp.zeros((8, 128), f32)
        for n, total in enumerate(dots):
            line = jnp.sum(total, axis=0, keepdims=True)
            acc = jnp.where(sub == n, jnp.broadcast_to(line, (8, 128)), acc)
        for s in (16, 32, 64):
            acc = acc + roll(acc, s, 1)
        return jnp.sum(jnp.where(sub == grp8, acc, 0.0), axis=0, keepdims=True)

    def exchange(src, dst, send_sem, recv_sem, targets):
        for k, target in enumerate(targets):
            pltpu.make_async_remote_copy(
                src_ref=src,
                dst_ref=dst.at[k],
                send_sem=send_sem,
                recv_sem=recv_sem,
                device_id=target,
                device_id_type=MESH,
            ).start()

    def start_sum(rnd, dots):
        own_a[rnd] = rows_of(dots)
        exchange(own_a.at[rnd], red_a.at[rnd], a_send.at[rnd], a_recv.at[rnd], plane_ids)

    def relay_sum(rnd):
        pltpu.make_async_copy(red_a.at[rnd], red_a.at[rnd], a_recv.at[rnd]).wait()
        own_b[rnd] = jnp.sum(red_a[rnd], axis=0) + own_a[rnd]
        exchange(own_b.at[rnd], red_b.at[rnd], b_send.at[rnd], b_recv.at[rnd], column_ids)

    def end_sum(rnd, count):
        pltpu.make_async_copy(red_b.at[rnd], red_b.at[rnd], b_recv.at[rnd]).wait()
        total = jnp.broadcast_to(jnp.sum(red_b[rnd], axis=0) + own_b[rnd], (8, 128))
        sums = []
        for n in range(count):
            one = jnp.where(grp8 == n, total, 0.0)
            for s in (16, 32, 64):
                one = one + roll(one, s, 1)
            sums.append(one)
        return sums

    def wide(coef):
        one = jnp.broadcast_to(coef[0:1], (64, 128))
        return jnp.concatenate([one, one], axis=1)

    def clear(f):
        for rnd in range(2):
            nbuf[rnd, f] = jnp.zeros((64, 128), f32)

    pl.when(dam == 0)(lambda: clear(0))
    pl.when(dam == ndam - 1)(lambda: clear(1))

    faces = onehot(z0, table_f[...], nn)
    part = coarse_own(0)
    fix = coarse_rest(0, part)
    faces = faces + fold(nn(fix, table_tf[...]))
    send_faces(0, faces)
    z0 = z0 + fold(nt(fix, table_t[...]))
    w0 = stiff(z0)
    corners = onehot(w0, table_c[...], nn)
    term = two(wait_faces(0, faces))
    put_corners(1, corners + fold(nt(term, table_fc[...])))
    copies = corner_copies(1)
    for copy in copies:
        copy.start()
    pending += copies
    w0 = w0 + fold(nt(term, table_f[...]))

    start_sum(0, [lump(r0 * z0), lump(z0 * w0)])
    q0 = smooth(w0)
    faces = onehot(q0, table_f[...], nn)
    part = coarse_own(1)
    fix = coarse_rest(1, part)
    faces = faces + fold(nn(fix, table_tf[...]))
    send_faces(1, faces)
    relay_sum(0)

    q0 = q0 + fold(nt(fix, table_t[...]))
    s0 = stiff(q0)
    gamma, delta = end_sum(0, 2)
    alpha = gamma / delta
    wide_alpha = wide(alpha)
    r1 = r0 - wide_alpha * w0
    z1 = z0 - wide_alpha * q0
    az = w0 - wide_alpha * s0
    face_alpha = jnp.concatenate([wide_alpha, wide_alpha], axis=1)
    faces_z = jnp.concatenate([gbuf[0, f] for f in range(4)], axis=1)
    faces_z1 = faces_z - face_alpha * faces
    rz, zz, zw = lump(r1 * z1), lump(z1 * az), lump(z1 * w0 + z0 * az)
    term = face_alpha * wait_faces(1, faces)
    start_sum(1, [rz, zz - lump(faces_z1 * term), zw - lump(faces_z * term)])

    @pl.when(dam >= 0)
    def _():
        fields[0], fields[1], fields[2], fields[4] = z0, z1, r1, w0
        fields[3] = az - fold(nt(two(term), table_f[...]))

    def turn(t, carry):
        for n in range(5):
            for h in range(2):
                turned[n, h, t] = swap8(fields[n, pl.ds(pl.multiple_of(8 * t, 8), 8), 128 * h : 128 * h + 128])
        return carry

    lax.fori_loop(0, 8, turn, 0)
    relay_sum(1)
    gnew, e_zz, e_zw = end_sum(1, 3)
    beta = gnew / gamma
    alpha1 = gnew / (e_zz + beta * (e_zw + beta * delta))
    scaled = alpha1 * beta
    for h in range(2):
        for t in range(8):
            at = (pl.ds(8 * h, 8), pl.ds(128 * t, 128))
            out_ref[(0,) + at] = (alpha + scaled) * turned[0, h, t] + alpha1 * turned[1, h, t]
            out_ref[(1,) + at] = turned[2, h, t] - alpha1 * turned[3, h, t] - scaled * turned[4, h, t]

    for copy in pending:
        copy.wait_send()
    for rnd in range(2):
        face_copy(rnd, 2).wait_send()
        face_copy(rnd, 3).wait_send()
        pl.when(below)(lambda: face_copy(rnd, 0).wait_send())
        pl.when(above)(lambda: face_copy(rnd, 1).wait_send())
    for rnd in range(2):
        pltpu.make_async_copy(red_a.at[rnd], red_a.at[rnd], a_send.at[rnd]).wait()
        pltpu.make_async_copy(red_b.at[rnd], red_b.at[rnd], b_send.at[rnd]).wait()


def solution(mesh):
    placed = (
        P("dam", "sec", None, None),
        P("dam", "sec", None, None),
        P("dam", "sec", None, None, None),
        P("dam", "sec", None, None),
        P("dam", "sec", None, None),
        P("dam", "sec", None, None, None),
        P("dam", "sec", None, None),
        P("dam", "sec", None, None),
        P("dam", "sec", None),
        P("dam", "sec", None),
    )
    dims = SPLITS[mesh.shape["dam"]] + (mesh.shape["sec"] // 2,)
    nx, nzl, ny, nzh = dims
    plane, column = nx * ny, nzl * nzh * 2

    def shards(load, mask, stiff, cols, cap, pre, fmap, fw, cmap, coarse):
        args = (
            load[0, 0], mask[0, 0], stiff[0, 0], cols.transpose(0, 3, 1, 2)[0], cap[0, 0],
            pre[0, 0], fmap[0, 0], fw[0, 0], cmap[0], coarse[0],
        )
        vmem = pltpu.VMEM
        dma = pltpu.SemaphoreType.DMA
        scratch = [vmem(a.shape, a.dtype) for a in args] + [
            vmem((1024, 512), bf16), vmem((1024, 512), bf16),
            vmem((1024, 64), bf16), vmem((1024, 64), bf16),
            vmem((512, 1536), bf16),
            vmem((256, 512), bf16), vmem((256, 128), bf16), vmem((256, 512), bf16),
            vmem((512, 512), bf16), vmem((128, 512), bf16),
            vmem((512, 64), f32), vmem((64, 512), f32),
            vmem((2, 512, 256), bf16), vmem((3, 512, 128), bf16),
            vmem((2, 2 * nzh, 32, 128), f32),
            vmem((2, 4, 64, 128), f32), vmem((2, 4, 64, 128), f32),
            vmem((2, 1, 128), f32), vmem((2, 1, 128), f32),
            vmem((2, plane - 1, 1, 128), f32), vmem((2, column - 1, 1, 128), f32),
            vmem((5, 64, 256), f32), vmem((5, 2, 8, 8, 128), f32),
            dma((10,)),
            dma((2, 2 * nzh - 1)), dma((2, nzh)),
            dma((2, 4)), dma((2, 4)),
            dma((2,)), dma((2,)), dma((2,)), dma((2,)),
        ]
        out = pl.pallas_call(
            functools.partial(kernel, dims),
            out_shape=jax.ShapeDtypeStruct((2, 16, 1024), f32),
            in_specs=[pl.BlockSpec(memory_space=pl.ANY)] * 10,
            out_specs=pl.BlockSpec(memory_space=pltpu.VMEM),
            scratch_shapes=scratch,
            compiler_params=pltpu.CompilerParams(
                collective_id=0, has_side_effects=True, vmem_limit_bytes=67043328
            ),
        )(*args)
        return out[0][None, None], out[1][None, None]

    return jax.shard_map(
        shards,
        mesh=mesh,
        in_specs=placed,
        out_specs=(P("dam", "sec", None, None), P("dam", "sec", None, None)),
        check_vma=False,
    )
```

```python
import functools

import jax
import jax.numpy as jnp
from jax import lax
from jax.experimental import pallas as pl
from jax.experimental.pallas import tpu as pltpu
from jax.sharding import PartitionSpec as P

MESH = pl.DeviceIdType.MESH
f32, bf16, i32 = jnp.float32, jnp.bfloat16, jnp.int32
HIGH = lax.Precision.HIGHEST

SPLITS = {128: (4, 4, 8), 8: (2, 2, 2), 4: (1, 2, 2), 2: (1, 1, 2)}


def iota(shape, dim):
    return lax.broadcasted_iota(i32, shape, dim)


def split(a):
    hi = a.astype(bf16)
    return hi, (a - hi.astype(f32)).astype(bf16)


def nn(a, b):
    return jnp.dot(a, b, preferred_element_type=f32)


def nt(a, b, precision=None):
    return lax.dot_general(
        a, b, (((1,), (1,)), ((), ())), precision=precision, preferred_element_type=f32
    )


def roll(a, amount, axis):
    return pltpu.roll(a, amount % a.shape[axis], axis)


def swap8(tile):
    sub, grp = iota((8, 128), 0), iota((8, 128), 1) // 16
    for s in (1, 2, 4):
        up = roll(roll(tile, 16 * s, 1), -s, 0)
        down = roll(roll(tile, -16 * s, 1), s, 0)
        tile = jnp.where(((sub ^ grp) & s) == 0, tile, jnp.where((grp & s) != 0, up, down))
    return tile


def onehot(field, table, product):
    hi, lo = split(field)
    both = product(jnp.concatenate([hi, lo], axis=0), table)
    half = field.shape[0]
    return both[:half] + both[half:]


def weights_of(field):
    hi, lo = split(field)
    return [
        jnp.concatenate([hi[:, h * 128 : h * 128 + 128], lo[:, h * 128 : h * 128 + 128]], axis=1)
        for h in range(2)
    ]


def block_apply(a_hi, a_lo, weights):
    grp = iota((64, 128), 1) // 16
    halves = []
    for h in range(2):
        rows = pl.ds(512 * h, 512)
        w = weights(h)
        one = nn(a_hi[rows, :], w)
        two = nn(a_lo[rows, :], w[:, :128])
        out = one[:, :128] + one[:, 128:] + two
        acc = out[:64]
        for b in range(1, 8):
            acc = jnp.where(grp == b, out[64 * b : 64 * b + 64], acc)
        halves.append(acc)
    return jnp.concatenate(halves, axis=1)


def kernel(
    dims, load_h, mask_h, stiff_h, cols_h, cap_h, pre_h, fmap_h, fw_h, cmap_h, coarse_h,
    out_ref,
    load_v, mask_v, stiff_v, cols_v, cap_v, pre_v, fmap_v, fw_v, cmap_v, coarse_v,
    k_hi, k_lo, p_hi, p_lo, cc, table_f, table_c, table_t, table_tf, table_fc, fw_rows, fw_full, wk, wc,
    ybuf, gbuf, nbuf, own_a, own_b, red_a, red_b, fields, turned,
    in_sem, y_send, y_recv, g_send, g_recv, a_send, a_recv, b_send, b_recv, word,
):
    nx, nzl, ny, nzh = dims
    plane, column = nx * ny, nzl * nzh * 2
    dam, sec = lax.axis_index("dam"), lax.axis_index("sec")
    ndam, nsec = nx * nzl * ny, nzh * 2
    xx, zl, yy = lax.div(dam, nzl * ny), lax.rem(lax.div(dam, ny), nzl), lax.rem(dam, ny)
    zh, core = lax.div(sec, 2), lax.rem(sec, 2)

    def turns(at, size):
        return [at] + [jnp.where(at + k < size, at + k, at + k - size) for k in range(1, size)]

    ring_y, ring_core = turns(yy, ny), turns(core, 2)
    ring_x = [x * (nzl * ny) for x in turns(xx, nx)]
    ring_zh = [z * 2 for z in turns(zh, nzh)]
    nz = nzh * nzl

    def far(k, size):
        return min(k, size - k)

    order = sorted(
        ((kx, ky) for kx in range(nx) for ky in range(ny)),
        key=lambda k: -far(k[0], nx) - far(k[1], ny),
    )[:-1]
    plane_ids = [(ring_x[kx] + zl * ny + ring_y[ky], sec) for kx, ky in order]
    column_ids = []
    ring_z = turns(zh * nzl + zl, nz)
    for k in sorted(range(nz), key=lambda k: -far(k, nz)):
        high = sum(jnp.where(ring_z[k] >= nzl * n, 1, 0) for n in range(1, nzh))
        along = ring_x[0] + (ring_z[k] - high * nzl) * ny + yy
        column_ids += [(along, high * 2 + c) for c in ring_core]
    column_ids = column_ids[:-2] + column_ids[-1:]

    face_ids = (
        (jnp.where(dam > 0, dam - 1, ndam - 1), sec),
        (jnp.where(dam < ndam - 1, dam + 1, 0), sec),
        (dam, jnp.where(sec > 0, sec - 1, nsec - 1)),
        (dam, jnp.where(sec < nsec - 1, sec + 1, 0)),
    )

    pairs = (
        (load_h, load_v), (mask_h, mask_v), (cmap_h, cmap_v), (pre_h, pre_v), (coarse_h, coarse_v),
        (fmap_h, fmap_v), (fw_h, fw_v), (cols_h, cols_v), (cap_h, cap_v), (stiff_h, stiff_v),
    )
    loads = [pltpu.make_async_copy(a, b, in_sem.at[n]) for n, (a, b) in enumerate(pairs)]
    for copy in loads[:3]:
        copy.start()

    barrier = pltpu.get_barrier_semaphore()

    def greet(target):
        pl.semaphore_signal(barrier, inc=1, device_id=target, device_id_type=MESH)

    below, above = dam > 0, dam < ndam - 1
    row, base = ring_x[0] + zl * ny, zl * ny + yy
    ring_l = [z * ny for z in turns(zl, nzl)]
    beside_y = [(row + ring_y[1], sec), (row + ring_y[-1], sec)]
    beside_x = [(ring_x[1] + base, sec), (ring_x[-1] + base, sec)]
    beside_l = [(ring_x[0] + ring_l[1] + yy, sec), (ring_x[0] + ring_l[-1] + yy, sec)]
    peers = [(dam, h + c) for h in ring_zh for c in ring_core][1:]
    near = peers[::-1] + beside_l + beside_x + beside_y
    for target in near:
        greet(target)
    pl.when(below)(lambda: greet(face_ids[0]))
    pl.when(above)(lambda: greet(face_ids[1]))
    for copy in loads[3:]:
        copy.start()

    lane = iota((8, 128), 1)
    grp8 = lane // 16

    loads[2].wait()
    loads[1].wait()
    loads[0].wait()
    row128 = iota((256, 128), 0)
    lane1, grp1 = iota((1, 128), 1), iota((1, 128), 1) // 16
    corner = cmap_v[...]
    where_c = jnp.zeros((1, 128), i32)
    for n in range(4):
        where_c = jnp.where(
            grp1 % 4 == n, jnp.broadcast_to(corner[:, n : n + 1], (1, 128)), where_c
        )
    target = where_c * 16 + lane1 % 16
    table_c[...] = jnp.where(row128 == jnp.broadcast_to(target, (256, 128)), 1.0, 0.0).astype(bf16)

    fan = jnp.where(iota((16, 128), 1) % 16 == iota((16, 128), 0), 1.0, 0.0)
    mask = nn(mask_v[...].astype(f32), fan)
    halves = []
    for h in range(2):
        m = mask[8 * h : 8 * h + 8]
        halves.append(
            jnp.concatenate(
                [
                    swap8(load_v[pl.ds(8 * h, 8), pl.ds(128 * t, 128)] * m)
                    for t in range(8)
                ],
                axis=0,
            )
        )
    r0 = jnp.concatenate(halves, axis=1)

    low = iota((32, 128), 1) < 64

    def corner_copies(rnd):
        def copy(dz, rc):
            return pltpu.make_async_remote_copy(
                src_ref=ybuf.at[rnd, sec],
                dst_ref=ybuf.at[rnd, sec],
                send_sem=y_send.at[rnd, 2 * dz + rc - 1],
                recv_sem=y_recv.at[rnd, dz],
                device_id=(dam, ring_zh[dz] + ring_core[rc]),
                device_id_type=MESH,
            )

        return [copy(dz, rc) for dz in range(1, nzh) for rc in range(2)] + [copy(0, 1)]

    def put_corners(rnd, both):
        ybuf[rnd, sec] = jnp.where(low, both[:32], both[32:])

    def coarse_weights(rnd, dz):
        chip = zh if dz == 0 else lax.div(ring_zh[nzh - dz], 2)
        first = iota((32, 128), 1) < 16
        for c in range(2):
            y = ybuf[rnd, 2 * chip + c]
            turned = [y if g == 0 else roll(y, -16 * g, 1) for g in range(8)]
            for n in range(4):
                for dh in range(2):
                    g = dh * 4 + n
                    hi = turned[g].astype(bf16).astype(f32)
                    prev = turned[(g + 7) % 8]
                    lo = prev - prev.astype(bf16).astype(f32)
                    wc[dz, pl.ds(c * 256 + n * 64 + dh * 32, 32), :] = jnp.where(first, hi, lo).astype(bf16)
        return pl.ds(pl.multiple_of(chip * 512, 512), 512)

    def wait_corners(rnd, dz):
        part = ybuf.at[rnd, pl.ds(0, 2 if dz else 1)]
        pltpu.make_async_copy(part, part, y_recv.at[rnd, dz]).wait()

    def coarse_own(rnd):
        wait_corners(rnd, 0)
        at = coarse_weights(rnd, 0)
        return nn(cc[:256, at], wc[0]) + nn(cc[256:, at], wc[0])

    def coarse_rest(rnd, out):
        for dz in range(1, nzh):
            wait_corners(rnd, dz)
        at = [coarse_weights(rnd, dz) for dz in range(1, nzh)]
        parts = [nn(cc[:256, a], wc[n + 1]) for n, a in enumerate(at)]
        parts += [nn(cc[256:, a], wc[n + 1]) for n, a in enumerate(at)]
        out = out + sum(parts[1:], parts[0])
        wide = jnp.concatenate([out[64 * n : 64 * n + 64] for n in range(4)], axis=1)
        hi, lo = split(wide)
        return jnp.concatenate([hi, lo], axis=0)

    def fold(both):
        return both[:64] + both[64:]

    def smooth(field):
        w = weights_of(field)
        return block_apply(p_hi, p_lo, lambda h: w[h])

    put_corners(0, onehot(r0, table_c[...], nn))
    copies = corner_copies(0)
    pl.semaphore_wait(barrier, len(near) + below.astype(i32) + above.astype(i32))
    for copy in copies:
        copy.start()

    def tell(n, targets):
        for target in targets:
            pl.semaphore_signal(word.at[n], inc=1, device_id=target, device_id_type=MESH)

    def hear(n, count):
        pl.semaphore_wait(word.at[n], count)

    tell(0, beside_y)
    tell(5, beside_l)

    loads[3].wait()
    for b in range(16):
        hi, lo = split(pre_v[b])
        p_hi[pl.ds(64 * b, 64), :] = hi
        p_lo[pl.ds(64 * b, 64), :] = lo
    z0 = smooth(r0)
    loads[4].wait()
    for n in range(4):
        hi, lo = split(coarse_v[pl.ds(64 * n, 64), :])
        cc[pl.ds(64 * n, 64), :] = hi
        cc[pl.ds(256 + 64 * n, 64), :] = lo
    for n in range(4):
        t = jnp.broadcast_to(corner[:, n : n + 1], (1, 128)) * 16 + lane1 % 16
        t = jnp.where(grp1 < 2, t, -1)
        table_t[:, pl.ds(128 * n, 128)] = jnp.where(
            row128 == jnp.broadcast_to(t, (256, 128)), 1.0, 0.0
        ).astype(bf16)
    loads[5].wait()
    fm = fmap_v[...]
    grp4 = iota((4, 128), 1) // 16
    where_f = jnp.zeros((4, 128), i32)
    for p in range(8):
        where_f = jnp.where(grp4 == p, jnp.broadcast_to(fm[:, p : p + 1], (4, 128)), where_f)
    where_f = where_f * 16 + iota((4, 128), 1) % 16
    for f in range(4):
        table_f[:, pl.ds(128 * f, 128)] = jnp.where(
            row128 == jnp.broadcast_to(where_f[f : f + 1], (256, 128)), 1.0, 0.0
        ).astype(bf16)
    modrow = iota((128, 128), 0) % 16
    rown = (iota((128, 128), 0) // 16) % 4
    early = iota((128, 128), 0) < 32
    for f in range(4):
        lanes = where_f[f : f + 1]
        match = jnp.zeros((128, 128), i32)
        for n in range(4):
            t = jnp.where(
                lanes // 16 == jnp.broadcast_to(corner[:, n : n + 1], (1, 128)), lane1 % 16, -1
            )
            t = jnp.broadcast_to(t, (128, 128))
            match = jnp.where(rown == n, t, match)
            table_tf[pl.ds(128 * n, 128), pl.ds(128 * f, 128)] = jnp.where(
                early, jnp.where(modrow == t, 1.0, 0.0), 0.0
            ).astype(bf16)
        table_fc[:, pl.ds(128 * f, 128)] = jnp.where(modrow == match, 1.0, 0.0).astype(bf16)
    hear(0, 2)
    tell(1, beside_y)
    hear(5, 2)
    tell(6, beside_l[:1])
    loads[6].wait()
    for f in range(4):
        for p in range(8):
            q = 8 * f + p
            fw_rows[pl.ds(16 * q, 16), :] = jnp.broadcast_to(
                fw_v[f : f + 1, 64 * p : 64 * p + 64], (16, 64)
            )
    eye = jnp.where(iota((64, 64), 0) == iota((64, 64), 1), 1.0, 0.0)
    fw_full[...] = nt(eye, fw_rows[...], HIGH)
    loads[7].wait()
    offsets = [
        jnp.broadcast_to(jnp.broadcast_to(cols_v[k][:, 0:1], (1, 128)), (64, 128)) for k in (1, 3, 5)
    ]
    loads[8].wait()
    place = jnp.where(iota((64, 128), 0) == iota((64, 128), 1), 1.0, 0.0)
    cap = jnp.dot(cap_v[...], place, precision=HIGH, preferred_element_type=f32)
    loads[9].wait()
    on_diag = iota((64, 128), 0) == iota((64, 128), 1)
    for b in range(16):
        rows = pl.ds(64 * b, 64)
        for t in range(4):
            wide = 128 if t < 3 else 64
            piece = stiff_v[b, :, 128 * t : 128 * t + wide]
            if t == 0:
                piece = piece + jnp.where(on_diag, jnp.broadcast_to(cap[b : b + 1], (64, 128)), 0.0)
            hi, lo = split(piece)
            k_hi[rows, 128 * t : 128 * t + wide] = hi
            k_lo[rows, 128 * t : 128 * t + wide] = lo
    k_hi[:, 448:512] = jnp.zeros((1024, 64), bf16)
    k_lo[:, 448:512] = jnp.zeros((1024, 64), bf16)
    for h in range(2):
        wk[h, 448:512, :] = jnp.zeros((64, 256), bf16)

    lane64 = iota((64, 128), 1)

    def shifted(field, bits, sign):
        a, b = field[:, :128], field[:, 128:]
        for s in (1, 2, 4):
            ra, rb = roll(a, -sign * 16 * s, 1), roll(b, -sign * 16 * s, 1)
            same = lane64 < 128 - 16 * s if sign > 0 else lane64 >= 16 * s
            na, nb = jnp.where(same, ra, rb), jnp.where(same, rb, ra)
            on = (bits & s) != 0
            a, b = jnp.where(on, na, a), jnp.where(on, nb, b)
        return jnp.concatenate([a, b], axis=1)

    def face_copy(rnd, f):
        return pltpu.make_async_remote_copy(
            src_ref=gbuf.at[rnd, f],
            dst_ref=nbuf.at[rnd, f ^ 1],
            send_sem=g_send.at[rnd, f],
            recv_sem=g_recv.at[rnd, f ^ 1],
            device_id=face_ids[f],
            device_id_type=MESH,
        )

    def send_faces(rnd, faces):
        for f in range(4):
            gbuf[rnd, f] = faces[:, 128 * f : 128 * f + 128]
        face_copy(rnd, 2).start()
        face_copy(rnd, 3).start()
        pl.when(below)(lambda: face_copy(rnd, 0).start())
        pl.when(above)(lambda: face_copy(rnd, 1).start())

    def stiff(field):
        chunks = [field]
        for bits in offsets:
            chunks += [shifted(field, bits, 1), shifted(field, bits, -1)]
        for k, chunk in enumerate(chunks):
            for h, w in enumerate(weights_of(chunk)):
                wk[h, pl.ds(64 * k, 64), :] = w
        return block_apply(k_hi, k_lo, lambda h: wk[h])

    def wait_faces(rnd, faces):
        pl.when(above)(lambda: face_copy(rnd, 0).wait_recv())
        pl.when(below)(lambda: face_copy(rnd, 1).wait_recv())
        face_copy(rnd, 2).wait_recv()
        face_copy(rnd, 3).wait_recv()
        beside = jnp.concatenate([nbuf[rnd, f] for f in range(4)], axis=1)
        return fw_full[...] * (faces - beside)

    def two(value):
        return jnp.concatenate(split(value), axis=0)

    def lump(prod):
        line = sum(prod[:, 128 * n : 128 * n + 128] for n in range(1, prod.shape[1] // 128))
        line = prod[:, :128] + line
        return sum((line[8 * t : 8 * t + 8] for t in range(1, 8)), line[:8])

    def rows_of(dots):
        sub = iota((8, 128), 0)
        acc = jnp.zeros((8, 128), f32)
        for n, total in enumerate(dots):
            line = jnp.sum(total, axis=0, keepdims=True)
            acc = jnp.where(sub == n, jnp.broadcast_to(line, (8, 128)), acc)
        for s in (16, 32, 64):
            acc = acc + roll(acc, s, 1)
        return jnp.sum(jnp.where(sub == grp8, acc, 0.0), axis=0, keepdims=True)

    def exchange(src, dst, send_sem, recv_sem, targets):
        for k, target in enumerate(targets):
            pltpu.make_async_remote_copy(
                src_ref=src,
                dst_ref=dst.at[k],
                send_sem=send_sem,
                recv_sem=recv_sem,
                device_id=target,
                device_id_type=MESH,
            ).start()

    def start_sum(rnd, dots):
        own_a[rnd] = rows_of(dots)
        exchange(own_a.at[rnd], red_a.at[rnd], a_send.at[rnd], a_recv.at[rnd], plane_ids)

    def relay_sum(rnd):
        pltpu.make_async_copy(red_a.at[rnd], red_a.at[rnd], a_recv.at[rnd]).wait()
        own_b[rnd] = jnp.sum(red_a[rnd], axis=0) + own_a[rnd]
        exchange(own_b.at[rnd], red_b.at[rnd], b_send.at[rnd], b_recv.at[rnd], column_ids)

    def end_sum(rnd, count):
        pltpu.make_async_copy(red_b.at[rnd], red_b.at[rnd], b_recv.at[rnd]).wait()
        total = jnp.broadcast_to(jnp.sum(red_b[rnd], axis=0) + own_b[rnd], (8, 128))
        sums = []
        for n in range(count):
            one = jnp.where(grp8 == n, total, 0.0)
            for s in (16, 32, 64):
                one = one + roll(one, s, 1)
            sums.append(one)
        return sums

    def wide(coef):
        one = jnp.broadcast_to(coef[0:1], (64, 128))
        return jnp.concatenate([one, one], axis=1)

    hear(1, 2)
    tell(2, beside_y)

    def clear(f):
        for rnd in range(2):
            nbuf[rnd, f] = jnp.zeros((64, 128), f32)

    pl.when(dam == 0)(lambda: clear(0))
    pl.when(dam == ndam - 1)(lambda: clear(1))

    faces = onehot(z0, table_f[...], nn)
    part = coarse_own(0)
    fix = coarse_rest(0, part)
    faces = faces + fold(nn(fix, table_tf[...]))
    send_faces(0, faces)
    hear(2, 2)
    tell(3, beside_x)
    z0 = z0 + fold(nt(fix, table_t[...]))
    w0 = stiff(z0)
    corners = onehot(w0, table_c[...], nn)
    hear(3, 2)
    tell(4, beside_x[:1])
    term = two(wait_faces(0, faces))
    put_corners(1, corners + fold(nt(term, table_fc[...])))
    copies = corner_copies(1)
    for copy in copies:
        copy.start()
    w0 = w0 + fold(nt(term, table_f[...]))

    hear(4, 1)
    hear(6, 1)
    start_sum(0, [lump(r0 * z0), lump(z0 * w0)])
    q0 = smooth(w0)
    faces = onehot(q0, table_f[...], nn)
    part = coarse_own(1)
    fix = coarse_rest(1, part)
    faces = faces + fold(nn(fix, table_tf[...]))
    send_faces(1, faces)
    relay_sum(0)

    q0 = q0 + fold(nt(fix, table_t[...]))
    s0 = stiff(q0)
    gamma, delta = end_sum(0, 2)
    alpha = gamma / delta
    wide_alpha = wide(alpha)
    r1 = r0 - wide_alpha * w0
    z1 = z0 - wide_alpha * q0
    az = w0 - wide_alpha * s0
    face_alpha = jnp.concatenate([wide_alpha, wide_alpha], axis=1)
    faces_z = jnp.concatenate([gbuf[0, f] for f in range(4)], axis=1)
    faces_z1 = faces_z - face_alpha * faces
    rz, zz, zw = lump(r1 * z1), lump(z1 * az), lump(z1 * w0 + z0 * az)
    term = face_alpha * wait_faces(1, faces)
    start_sum(1, [rz, zz - lump(faces_z1 * term), zw - lump(faces_z * term)])

    @pl.when(dam >= 0)
    def _():
        fields[0], fields[1], fields[2], fields[4] = z0, z1, r1, w0
        fields[3] = az - fold(nt(two(term), table_f[...]))

    def turn(t, carry):
        for n in range(5):
            for h in range(2):
                turned[n, h, t] = swap8(fields[n, pl.ds(pl.multiple_of(8 * t, 8), 8), 128 * h : 128 * h + 128])
        return carry

    lax.fori_loop(0, 8, turn, 0)
    for rnd in range(2):
        for copy in corner_copies(rnd):
            copy.wait_send()
        face_copy(rnd, 2).wait_send()
        face_copy(rnd, 3).wait_send()
        pl.when(below)(lambda: face_copy(rnd, 0).wait_send())
        pl.when(above)(lambda: face_copy(rnd, 1).wait_send())
    pltpu.make_async_copy(red_a.at[0], red_a.at[0], a_send.at[0]).wait()
    pltpu.make_async_copy(red_b.at[0], red_b.at[0], b_send.at[0]).wait()
    relay_sum(1)
    gnew, e_zz, e_zw = end_sum(1, 3)
    beta = gnew / gamma
    alpha1 = gnew / (e_zz + beta * (e_zw + beta * delta))
    scaled = alpha1 * beta
    for h in range(2):
        for t in range(8):
            at = (pl.ds(8 * h, 8), pl.ds(128 * t, 128))
            out_ref[(0,) + at] = (alpha + scaled) * turned[0, h, t] + alpha1 * turned[1, h, t]
            out_ref[(1,) + at] = turned[2, h, t] - alpha1 * turned[3, h, t] - scaled * turned[4, h, t]

    pltpu.make_async_copy(red_a.at[1], red_a.at[1], a_send.at[1]).wait()
    pltpu.make_async_copy(red_b.at[1], red_b.at[1], b_send.at[1]).wait()


def solution(mesh):
    placed = (
        P("dam", "sec", None, None),
        P("dam", "sec", None, None),
        P("dam", "sec", None, None, None),
        P("dam", "sec", None, None),
        P("dam", "sec", None, None),
        P("dam", "sec", None, None, None),
        P("dam", "sec", None, None),
        P("dam", "sec", None, None),
        P("dam", "sec", None),
        P("dam", "sec", None),
    )
    dims = SPLITS[mesh.shape["dam"]] + (mesh.shape["sec"] // 2,)
    nx, nzl, ny, nzh = dims
    plane, column = nx * ny, nzl * nzh * 2

    def shards(load, mask, stiff, cols, cap, pre, fmap, fw, cmap, coarse):
        args = (
            load[0, 0], mask[0, 0], stiff[0, 0], cols.transpose(0, 3, 1, 2)[0], cap[0, 0],
            pre[0, 0], fmap[0, 0], fw[0, 0], cmap[0], coarse[0],
        )
        vmem = pltpu.VMEM
        dma = pltpu.SemaphoreType.DMA
        scratch = [vmem(a.shape, a.dtype) for a in args] + [
            vmem((1024, 512), bf16), vmem((1024, 512), bf16),
            vmem((1024, 64), bf16), vmem((1024, 64), bf16),
            vmem((512, 1536), bf16),
            vmem((256, 512), bf16), vmem((256, 128), bf16), vmem((256, 512), bf16),
            vmem((512, 512), bf16), vmem((128, 512), bf16),
            vmem((512, 64), f32), vmem((64, 512), f32),
            vmem((2, 512, 256), bf16), vmem((3, 512, 128), bf16),
            vmem((2, 2 * nzh, 32, 128), f32),
            vmem((2, 4, 64, 128), f32), vmem((2, 4, 64, 128), f32),
            vmem((2, 1, 128), f32), vmem((2, 1, 128), f32),
            vmem((2, plane - 1, 1, 128), f32), vmem((2, column - 1, 1, 128), f32),
            vmem((5, 64, 256), f32), vmem((5, 2, 8, 8, 128), f32),
            dma((10,)),
            dma((2, 2 * nzh - 1)), dma((2, nzh)),
            dma((2, 4)), dma((2, 4)),
            dma((2,)), dma((2,)), dma((2,)), dma((2,)),
            pltpu.SemaphoreType.REGULAR((7,)),
        ]
        out = pl.pallas_call(
            functools.partial(kernel, dims),
            out_shape=jax.ShapeDtypeStruct((2, 16, 1024), f32),
            in_specs=[pl.BlockSpec(memory_space=pl.ANY)] * 10,
            out_specs=pl.BlockSpec(memory_space=pltpu.VMEM),
            scratch_shapes=scratch,
            compiler_params=pltpu.CompilerParams(
                collective_id=0, has_side_effects=True, vmem_limit_bytes=67043328
            ),
        )(*args)
        return out[0][None, None], out[1][None, None]

    return jax.shard_map(
        shards,
        mesh=mesh,
        in_specs=placed,
        out_specs=(P("dam", "sec", None, None), P("dam", "sec", None, None)),
        check_vma=False,
    )
```

```python
import functools

import jax
import jax.numpy as jnp
from jax import lax
from jax.experimental import pallas as pl
from jax.experimental.pallas import tpu as pltpu
from jax.sharding import PartitionSpec as P

MESH = pl.DeviceIdType.MESH
f32, bf16, i32 = jnp.float32, jnp.bfloat16, jnp.int32
HIGH = lax.Precision.HIGHEST

SPLITS = {128: (4, 4, 8), 8: (2, 2, 2), 4: (1, 2, 2), 2: (1, 1, 2)}


def iota(shape, dim):
    return lax.broadcasted_iota(i32, shape, dim)


def split(a):
    hi = a.astype(bf16)
    return hi, (a - hi.astype(f32)).astype(bf16)


def nn(a, b):
    return jnp.dot(a, b, preferred_element_type=f32)


def nt(a, b, precision=None):
    return lax.dot_general(
        a, b, (((1,), (1,)), ((), ())), precision=precision, preferred_element_type=f32
    )


def roll(a, amount, axis):
    return pltpu.roll(a, amount % a.shape[axis], axis)


def swap8(tile):
    sub, grp = iota((8, 128), 0), iota((8, 128), 1) // 16
    for s in (1, 2, 4):
        up = roll(roll(tile, 16 * s, 1), -s, 0)
        down = roll(roll(tile, -16 * s, 1), s, 0)
        tile = jnp.where(((sub ^ grp) & s) == 0, tile, jnp.where((grp & s) != 0, up, down))
    return tile


def onehot(field, table, product):
    hi, lo = split(field)
    both = product(jnp.concatenate([hi, lo], axis=0), table)
    half = field.shape[0]
    return both[:half] + both[half:]


def weights_of(field):
    hi, lo = split(field)
    return [
        jnp.concatenate([hi[:, h * 128 : h * 128 + 128], lo[:, h * 128 : h * 128 + 128]], axis=1)
        for h in range(2)
    ]


def block_apply(a_hi, a_lo, weights):
    grp = iota((64, 128), 1) // 16
    halves = []
    for h in range(2):
        rows = pl.ds(512 * h, 512)
        w = weights(h)
        one = nn(a_hi[rows, :], w)
        two = nn(a_lo[rows, :], w[:, :128])
        out = one[:, :128] + one[:, 128:] + two
        acc = out[:64]
        for b in range(1, 8):
            acc = jnp.where(grp == b, out[64 * b : 64 * b + 64], acc)
        halves.append(acc)
    return jnp.concatenate(halves, axis=1)


def kernel(
    dims, load_h, mask_h, stiff_h, cols_h, cap_h, pre_h, fmap_h, fw_h, cmap_h, coarse_h,
    out_ref,
    load_v, mask_v, stiff_v, cols_v, cap_v, pre_v, fmap_v, fw_v, cmap_v, coarse_v,
    k_hi, k_lo, p_hi, p_lo, cc, table_f, table_c, table_t, table_tf, table_fc, fw_rows, fw_full, wk, wc,
    ybuf, gbuf, nbuf, own_a, own_b, red_a, red_b, fields, turned,
    in_sem, y_send, y_recv, g_recv, a_send, a_recv, b_send, b_recv, word,
):
    nx, nzl, ny, nzh = dims
    plane, column = nx * ny, nzl * nzh * 2
    dam, sec = lax.axis_index("dam"), lax.axis_index("sec")
    ndam, nsec = nx * nzl * ny, nzh * 2
    xx, zl, yy = lax.div(dam, nzl * ny), lax.rem(lax.div(dam, ny), nzl), lax.rem(dam, ny)
    zh, core = lax.div(sec, 2), lax.rem(sec, 2)

    def turns(at, size):
        return [at] + [jnp.where(at + k < size, at + k, at + k - size) for k in range(1, size)]

    ring_y, ring_core = turns(yy, ny), turns(core, 2)
    ring_x = [x * (nzl * ny) for x in turns(xx, nx)]
    ring_zh = [z * 2 for z in turns(zh, nzh)]
    face_ids = (
        (jnp.where(dam > 0, dam - 1, ndam - 1), sec),
        (jnp.where(dam < ndam - 1, dam + 1, 0), sec),
        (dam, jnp.where(sec > 0, sec - 1, nsec - 1)),
        (dam, jnp.where(sec < nsec - 1, sec + 1, 0)),
    )

    pairs = (
        (load_h, load_v), (mask_h, mask_v), (cmap_h, cmap_v), (pre_h, pre_v), (coarse_h, coarse_v),
        (fmap_h, fmap_v), (fw_h, fw_v), (cols_h, cols_v), (cap_h, cap_v), (stiff_h, stiff_v),
    )
    loads = [pltpu.make_async_copy(a, b, in_sem.at[n]) for n, (a, b) in enumerate(pairs)]
    for copy in loads[:3]:
        copy.start()

    barrier = pltpu.get_barrier_semaphore()

    def greet(target):
        pl.semaphore_signal(barrier, inc=1, device_id=target, device_id_type=MESH)

    below, above = dam > 0, dam < ndam - 1
    row, base = ring_x[0] + zl * ny, zl * ny + yy
    ring_l = [z * ny for z in turns(zl, nzl)]
    beside_y = [(row + ring_y[1], sec), (row + ring_y[-1], sec)]
    beside_x = [(ring_x[1] + base, sec), (ring_x[-1] + base, sec)]
    beside_l = [(ring_x[0] + ring_l[1] + yy, sec), (ring_x[0] + ring_l[-1] + yy, sec)]
    peers = [(dam, h + c) for h in ring_zh for c in ring_core][1:]
    near = peers[::-1] + beside_l + beside_x + beside_y
    for target in near:
        greet(target)
    pl.when(below)(lambda: greet(face_ids[0]))
    pl.when(above)(lambda: greet(face_ids[1]))
    for copy in loads[3:]:
        copy.start()

    lane = iota((8, 128), 1)
    grp8 = lane // 16

    loads[2].wait()
    loads[1].wait()
    loads[0].wait()
    row128 = iota((256, 128), 0)
    lane1, grp1 = iota((1, 128), 1), iota((1, 128), 1) // 16
    corner = cmap_v[...]
    where_c = jnp.zeros((1, 128), i32)
    for n in range(4):
        where_c = jnp.where(
            grp1 % 4 == n, jnp.broadcast_to(corner[:, n : n + 1], (1, 128)), where_c
        )
    target = where_c * 16 + lane1 % 16
    table_c[...] = jnp.where(row128 == jnp.broadcast_to(target, (256, 128)), 1.0, 0.0).astype(bf16)

    fan = jnp.where(iota((16, 128), 1) % 16 == iota((16, 128), 0), 1.0, 0.0)
    mask = nn(mask_v[...].astype(f32), fan)
    halves = []
    for h in range(2):
        m = mask[8 * h : 8 * h + 8]
        halves.append(
            jnp.concatenate(
                [
                    swap8(load_v[pl.ds(8 * h, 8), pl.ds(128 * t, 128)] * m)
                    for t in range(8)
                ],
                axis=0,
            )
        )
    r0 = jnp.concatenate(halves, axis=1)

    low = iota((32, 128), 1) < 64

    def corner_copies(rnd):
        def copy(dz, rc):
            return pltpu.make_async_remote_copy(
                src_ref=ybuf.at[rnd, sec],
                dst_ref=ybuf.at[rnd, sec],
                send_sem=y_send.at[rnd, 2 * dz + rc - 1],
                recv_sem=y_recv.at[rnd, dz],
                device_id=(dam, ring_zh[dz] + ring_core[rc]),
                device_id_type=MESH,
            )

        return [copy(dz, rc) for dz in range(1, nzh) for rc in range(2)] + [copy(0, 1)]

    def put_corners(rnd, both):
        ybuf[rnd, sec] = jnp.where(low, both[:32], both[32:])

    def coarse_weights(rnd, dz):
        chip = zh if dz == 0 else lax.div(ring_zh[nzh - dz], 2)
        first = iota((32, 128), 1) < 16
        for c in range(2):
            y = ybuf[rnd, 2 * chip + c]
            turned = [y if g == 0 else roll(y, -16 * g, 1) for g in range(8)]
            for n in range(4):
                for dh in range(2):
                    g = dh * 4 + n
                    hi = turned[g].astype(bf16).astype(f32)
                    prev = turned[(g + 7) % 8]
                    lo = prev - prev.astype(bf16).astype(f32)
                    wc[dz, pl.ds(c * 256 + n * 64 + dh * 32, 32), :] = jnp.where(first, hi, lo).astype(bf16)
        return pl.ds(pl.multiple_of(chip * 512, 512), 512)

    def wait_corners(rnd, dz):
        part = ybuf.at[rnd, pl.ds(0, 2 if dz else 1)]
        pltpu.make_async_copy(part, part, y_recv.at[rnd, dz]).wait()

    def coarse_own(rnd):
        wait_corners(rnd, 0)
        at = coarse_weights(rnd, 0)
        return nn(cc[:256, at], wc[0]) + nn(cc[256:, at], wc[0])

    def coarse_rest(rnd, out):
        for dz in range(1, nzh):
            wait_corners(rnd, dz)
        at = [coarse_weights(rnd, dz) for dz in range(1, nzh)]
        w = jnp.concatenate([wc[dz] for dz in range(1, nzh)], axis=0)
        for rows in (pl.ds(0, 256), pl.ds(256, 256)):
            out = out + nn(jnp.concatenate([cc[rows, a] for a in at], axis=1), w)
        wide = jnp.concatenate([out[64 * n : 64 * n + 64] for n in range(4)], axis=1)
        hi, lo = split(wide)
        return jnp.concatenate([hi, lo], axis=0)

    def fold(both):
        return both[:64] + both[64:]

    def smooth(field):
        w = weights_of(field)
        return block_apply(p_hi, p_lo, lambda h: w[h])

    put_corners(0, onehot(r0, table_c[...], nn))
    copies = corner_copies(0)
    pl.semaphore_wait(barrier, len(near) + below.astype(i32) + above.astype(i32))
    for copy in copies:
        copy.start()

    def tell(n, targets):
        for target in targets:
            pl.semaphore_signal(word.at[n], inc=1, device_id=target, device_id_type=MESH)

    def hear(n, count):
        pl.semaphore_wait(word.at[n], count)

    tell(0, beside_y)
    tell(5, beside_l)

    nz = nzh * nzl

    def far(k, size):
        return min(k, size - k)

    order = sorted(
        ((kx, ky) for kx in range(nx) for ky in range(ny)),
        key=lambda k: -far(k[0], nx) - far(k[1], ny),
    )[:-1]
    plane_ids = [(ring_x[kx] + zl * ny + ring_y[ky], sec) for kx, ky in order]
    column_ids = []
    ring_z = turns(zh * nzl + zl, nz)
    for k in sorted(range(nz), key=lambda k: -far(k, nz)):
        high = sum(jnp.where(ring_z[k] >= nzl * n, 1, 0) for n in range(1, nzh))
        along = ring_x[0] + (ring_z[k] - high * nzl) * ny + yy
        column_ids += [(along, high * 2 + c) for c in ring_core]
    column_ids = column_ids[:-2] + column_ids[-1:]

    loads[3].wait()
    for b in range(16):
        hi, lo = split(pre_v[b])
        p_hi[pl.ds(64 * b, 64), :] = hi
        p_lo[pl.ds(64 * b, 64), :] = lo
    z0 = smooth(r0)
    loads[4].wait()
    for n in range(4):
        hi, lo = split(coarse_v[pl.ds(64 * n, 64), :])
        cc[pl.ds(64 * n, 64), :] = hi
        cc[pl.ds(256 + 64 * n, 64), :] = lo
    for n in range(4):
        t = jnp.broadcast_to(corner[:, n : n + 1], (1, 128)) * 16 + lane1 % 16
        t = jnp.where(grp1 < 2, t, -1)
        table_t[:, pl.ds(128 * n, 128)] = jnp.where(
            row128 == jnp.broadcast_to(t, (256, 128)), 1.0, 0.0
        ).astype(bf16)
    loads[5].wait()
    fm = fmap_v[...]
    grp4 = iota((4, 128), 1) // 16
    where_f = jnp.zeros((4, 128), i32)
    for p in range(8):
        where_f = jnp.where(grp4 == p, jnp.broadcast_to(fm[:, p : p + 1], (4, 128)), where_f)
    where_f = where_f * 16 + iota((4, 128), 1) % 16
    for f in range(4):
        table_f[:, pl.ds(128 * f, 128)] = jnp.where(
            row128 == jnp.broadcast_to(where_f[f : f + 1], (256, 128)), 1.0, 0.0
        ).astype(bf16)
    modrow = iota((128, 128), 0) % 16
    rown = (iota((128, 128), 0) // 16) % 4
    early = iota((128, 128), 0) < 32
    for f in range(4):
        lanes = where_f[f : f + 1]
        match = jnp.zeros((128, 128), i32)
        for n in range(4):
            t = jnp.where(
                lanes // 16 == jnp.broadcast_to(corner[:, n : n + 1], (1, 128)), lane1 % 16, -1
            )
            t = jnp.broadcast_to(t, (128, 128))
            match = jnp.where(rown == n, t, match)
            table_tf[pl.ds(128 * n, 128), pl.ds(128 * f, 128)] = jnp.where(
                early, jnp.where(modrow == t, 1.0, 0.0), 0.0
            ).astype(bf16)
        table_fc[:, pl.ds(128 * f, 128)] = jnp.where(modrow == match, 1.0, 0.0).astype(bf16)
    hear(0, 2)
    tell(1, beside_y)
    hear(5, 2)
    tell(6, beside_l[:1])
    loads[6].wait()
    for f in range(4):
        for p in range(8):
            q = 8 * f + p
            fw_rows[pl.ds(16 * q, 16), :] = jnp.broadcast_to(
                fw_v[f : f + 1, 64 * p : 64 * p + 64], (16, 64)
            )
    eye = jnp.where(iota((64, 64), 0) == iota((64, 64), 1), 1.0, 0.0)
    fw_full[...] = nt(eye, fw_rows[...], HIGH)
    loads[7].wait()
    offsets = [
        jnp.broadcast_to(jnp.broadcast_to(cols_v[k][:, 0:1], (1, 128)), (64, 128)) for k in (1, 3, 5)
    ]
    loads[8].wait()
    place = jnp.where(iota((64, 128), 0) == iota((64, 128), 1), 1.0, 0.0)
    cap = jnp.dot(cap_v[...], place, precision=HIGH, preferred_element_type=f32)
    loads[9].wait()
    on_diag = iota((64, 128), 0) == iota((64, 128), 1)
    for b in range(16):
        rows = pl.ds(64 * b, 64)
        for t in range(4):
            wide = 128 if t < 3 else 64
            piece = stiff_v[b, :, 128 * t : 128 * t + wide]
            if t == 0:
                piece = piece + jnp.where(on_diag, jnp.broadcast_to(cap[b : b + 1], (64, 128)), 0.0)
            hi, lo = split(piece)
            k_hi[rows, 128 * t : 128 * t + wide] = hi
            k_lo[rows, 128 * t : 128 * t + wide] = lo
    k_hi[:, 448:512] = jnp.zeros((1024, 64), bf16)
    k_lo[:, 448:512] = jnp.zeros((1024, 64), bf16)
    for h in range(2):
        wk[h, 448:512, :] = jnp.zeros((64, 256), bf16)

    lane64 = iota((64, 128), 1)

    def shifted(field, bits, sign):
        a, b = field[:, :128], field[:, 128:]
        for s in (1, 2, 4):
            ra, rb = roll(a, -sign * 16 * s, 1), roll(b, -sign * 16 * s, 1)
            same = lane64 < 128 - 16 * s if sign > 0 else lane64 >= 16 * s
            na, nb = jnp.where(same, ra, rb), jnp.where(same, rb, ra)
            on = (bits & s) != 0
            a, b = jnp.where(on, na, a), jnp.where(on, nb, b)
        return jnp.concatenate([a, b], axis=1)

    def face_copy(rnd, f):
        return pltpu.make_async_remote_copy(
            src_ref=gbuf.at[rnd, f],
            dst_ref=nbuf.at[rnd, f ^ 1],
            send_sem=in_sem.at[4 * rnd + f],
            recv_sem=g_recv.at[rnd, f ^ 1],
            device_id=face_ids[f],
            device_id_type=MESH,
        )

    def send_faces(rnd, faces):
        for f in range(4):
            gbuf[rnd, f] = faces[:, 128 * f : 128 * f + 128]
        face_copy(rnd, 2).start()
        face_copy(rnd, 3).start()
        pl.when(below)(lambda: face_copy(rnd, 0).start())
        pl.when(above)(lambda: face_copy(rnd, 1).start())

    def stiff(field):
        chunks = [field]
        for bits in offsets:
            chunks += [shifted(field, bits, 1), shifted(field, bits, -1)]
        for k, chunk in enumerate(chunks):
            for h, w in enumerate(weights_of(chunk)):
                wk[h, pl.ds(64 * k, 64), :] = w
        return block_apply(k_hi, k_lo, lambda h: wk[h])

    def wait_faces(rnd, faces):
        pl.when(above)(lambda: face_copy(rnd, 0).wait_recv())
        pl.when(below)(lambda: face_copy(rnd, 1).wait_recv())
        face_copy(rnd, 2).wait_recv()
        face_copy(rnd, 3).wait_recv()
        beside = jnp.concatenate([nbuf[rnd, f] for f in range(4)], axis=1)
        return fw_full[...] * (faces - beside)

    def two(value):
        return jnp.concatenate(split(value), axis=0)

    def lump(prod):
        line = sum(prod[:, 128 * n : 128 * n + 128] for n in range(1, prod.shape[1] // 128))
        line = prod[:, :128] + line
        return sum((line[8 * t : 8 * t + 8] for t in range(1, 8)), line[:8])

    def rows_of(dots):
        sub = iota((8, 128), 0)
        acc = jnp.zeros((8, 128), f32)
        for n, total in enumerate(dots):
            line = jnp.sum(total, axis=0, keepdims=True)
            acc = jnp.where(sub == n, jnp.broadcast_to(line, (8, 128)), acc)
        for s in (16, 32, 64):
            acc = acc + roll(acc, s, 1)
        return jnp.sum(jnp.where(sub == grp8, acc, 0.0), axis=0, keepdims=True)

    def exchange(src, dst, send_sem, recv_sem, targets):
        for k, target in enumerate(targets):
            pltpu.make_async_remote_copy(
                src_ref=src,
                dst_ref=dst.at[k],
                send_sem=send_sem,
                recv_sem=recv_sem,
                device_id=target,
                device_id_type=MESH,
            ).start()

    def start_sum(rnd, dots):
        own_a[rnd] = rows_of(dots)
        exchange(own_a.at[rnd], red_a.at[rnd], a_send.at[rnd], a_recv.at[rnd], plane_ids)

    def relay_sum(rnd):
        pltpu.make_async_copy(red_a.at[rnd], red_a.at[rnd], a_recv.at[rnd]).wait()
        own_b[rnd] = jnp.sum(red_a[rnd], axis=0) + own_a[rnd]
        exchange(own_b.at[rnd], red_b.at[rnd], b_send.at[rnd], b_recv.at[rnd], column_ids)

    def end_sum(rnd, count):
        pltpu.make_async_copy(red_b.at[rnd], red_b.at[rnd], b_recv.at[rnd]).wait()
        total = jnp.broadcast_to(jnp.sum(red_b[rnd], axis=0) + own_b[rnd], (8, 128))
        sums = []
        for n in range(count):
            one = jnp.where(grp8 == n, total, 0.0)
            for s in (16, 32, 64):
                one = one + roll(one, s, 1)
            sums.append(one)
        return sums

    def wide(coef):
        one = jnp.broadcast_to(coef[0:1], (64, 128))
        return jnp.concatenate([one, one], axis=1)

    hear(1, 2)
    tell(2, beside_y)

    def clear(f):
        for rnd in range(2):
            nbuf[rnd, f] = jnp.zeros((64, 128), f32)

    pl.when(dam == 0)(lambda: clear(0))
    pl.when(dam == ndam - 1)(lambda: clear(1))

    faces = onehot(z0, table_f[...], nn)
    part = coarse_own(0)
    fix = coarse_rest(0, part)
    faces = faces + fold(nn(fix, table_tf[...]))
    send_faces(0, faces)
    hear(2, 2)
    tell(3, beside_x)
    z0 = z0 + fold(nt(fix, table_t[...]))
    w0 = stiff(z0)
    corners = onehot(w0, table_c[...], nn)
    hear(3, 2)
    tell(4, beside_x[:1])
    term = two(wait_faces(0, faces))
    put_corners(1, corners + fold(nt(term, table_fc[...])))
    copies = corner_copies(1)
    for copy in copies:
        copy.start()
    w0 = w0 + fold(nt(term, table_f[...]))

    hear(4, 1)
    hear(6, 1)
    start_sum(0, [lump(r0 * z0), lump(z0 * w0)])
    q0 = smooth(w0)
    faces = onehot(q0, table_f[...], nn)
    part = coarse_own(1)
    fix = coarse_rest(1, part)
    faces = faces + fold(nn(fix, table_tf[...]))
    send_faces(1, faces)
    relay_sum(0)

    q0 = q0 + fold(nt(fix, table_t[...]))
    s0 = stiff(q0)
    gamma, delta = end_sum(0, 2)
    alpha = gamma / delta
    wide_alpha = wide(alpha)
    r1 = r0 - wide_alpha * w0
    z1 = z0 - wide_alpha * q0
    az = w0 - wide_alpha * s0
    face_alpha = jnp.concatenate([wide_alpha, wide_alpha], axis=1)
    faces_z = jnp.concatenate([gbuf[0, f] for f in range(4)], axis=1)
    faces_z1 = faces_z - face_alpha * faces
    rz, zz, zw = lump(r1 * z1), lump(z1 * az), lump(z1 * w0 + z0 * az)
    term = face_alpha * wait_faces(1, faces)
    start_sum(1, [rz, zz - lump(faces_z1 * term), zw - lump(faces_z * term)])

    @pl.when(dam >= 0)
    def _():
        fields[0], fields[1], fields[2], fields[4] = z0, z1, r1, w0
        fields[3] = az - fold(nt(two(term), table_f[...]))

    def turn(t, carry):
        for n in range(5):
            for h in range(2):
                turned[n, h, t] = swap8(fields[n, pl.ds(pl.multiple_of(8 * t, 8), 8), 128 * h : 128 * h + 128])
        return carry

    lax.fori_loop(0, 8, turn, 0)
    for rnd in range(2):
        for copy in corner_copies(rnd):
            copy.wait_send()
        face_copy(rnd, 2).wait_send()
        face_copy(rnd, 3).wait_send()
        pl.when(below)(lambda: face_copy(rnd, 0).wait_send())
        pl.when(above)(lambda: face_copy(rnd, 1).wait_send())
    pltpu.make_async_copy(red_a.at[0], red_a.at[0], a_send.at[0]).wait()
    pltpu.make_async_copy(red_b.at[0], red_b.at[0], b_send.at[0]).wait()
    relay_sum(1)
    gnew, e_zz, e_zw = end_sum(1, 3)
    beta = gnew / gamma
    alpha1 = gnew / (e_zz + beta * (e_zw + beta * delta))
    scaled = alpha1 * beta
    for h in range(2):
        for t in range(8):
            at = (pl.ds(8 * h, 8), pl.ds(128 * t, 128))
            out_ref[(0,) + at] = (alpha + scaled) * turned[0, h, t] + alpha1 * turned[1, h, t]
            out_ref[(1,) + at] = turned[2, h, t] - alpha1 * turned[3, h, t] - scaled * turned[4, h, t]

    pltpu.make_async_copy(red_a.at[1], red_a.at[1], a_send.at[1]).wait()
    pltpu.make_async_copy(red_b.at[1], red_b.at[1], b_send.at[1]).wait()


def solution(mesh):
    placed = (
        P("dam", "sec", None, None),
        P("dam", "sec", None, None),
        P("dam", "sec", None, None, None),
        P("dam", "sec", None, None),
        P("dam", "sec", None, None),
        P("dam", "sec", None, None, None),
        P("dam", "sec", None, None),
        P("dam", "sec", None, None),
        P("dam", "sec", None),
        P("dam", "sec", None),
    )
    dims = SPLITS[mesh.shape["dam"]] + (mesh.shape["sec"] // 2,)
    nx, nzl, ny, nzh = dims
    plane, column = nx * ny, nzl * nzh * 2

    def shards(load, mask, stiff, cols, cap, pre, fmap, fw, cmap, coarse):
        args = (
            load[0, 0], mask[0, 0], stiff[0, 0], cols.transpose(0, 3, 1, 2)[0], cap[0, 0],
            pre[0, 0], fmap[0, 0], fw[0, 0], cmap[0], coarse[0],
        )
        vmem = pltpu.VMEM
        dma = pltpu.SemaphoreType.DMA
        scratch = [vmem(a.shape, a.dtype) for a in args] + [
            vmem((1024, 512), bf16), vmem((1024, 512), bf16),
            vmem((1024, 64), bf16), vmem((1024, 64), bf16),
            vmem((512, 1536), bf16),
            vmem((256, 512), bf16), vmem((256, 128), bf16), vmem((256, 512), bf16),
            vmem((512, 512), bf16), vmem((128, 512), bf16),
            vmem((512, 64), f32), vmem((64, 512), f32),
            vmem((2, 512, 256), bf16), vmem((3, 512, 128), bf16),
            vmem((2, 2 * nzh, 32, 128), f32),
            vmem((2, 4, 64, 128), f32), vmem((2, 4, 64, 128), f32),
            vmem((2, 1, 128), f32), vmem((2, 1, 128), f32),
            vmem((2, plane - 1, 1, 128), f32), vmem((2, column - 1, 1, 128), f32),
            vmem((5, 64, 256), f32), vmem((5, 2, 8, 8, 128), f32),
            dma((10,)),
            dma((2, 2 * nzh - 1)), dma((2, nzh)),
            dma((2, 4)),
            dma((2,)), dma((2,)), dma((2,)), dma((2,)),
            pltpu.SemaphoreType.REGULAR((7,)),
        ]
        out = pl.pallas_call(
            functools.partial(kernel, dims),
            out_shape=jax.ShapeDtypeStruct((2, 16, 1024), f32),
            in_specs=[pl.BlockSpec(memory_space=pl.ANY)] * 10,
            out_specs=pl.BlockSpec(memory_space=pltpu.VMEM),
            scratch_shapes=scratch,
            compiler_params=pltpu.CompilerParams(
                collective_id=0, has_side_effects=True, vmem_limit_bytes=67043328
            ),
        )(*args)
        return out[0][None, None], out[1][None, None]

    return jax.shard_map(
        shards,
        mesh=mesh,
        in_specs=placed,
        out_specs=(P("dam", "sec", None, None), P("dam", "sec", None, None)),
        check_vma=False,
    )
```
